512 devices in a mesh: seq: 32 (over x_lo, z), head: 4 (over y), dp: 4 (over x_hi, core).
Axes of the slice: x: 4 (x_hi: 2, x_lo: 2; x = x_hi * 2 + x_lo), y: 4, z: 16, core: 2. Of those that a mesh axis runs over, the one named last changes fastest.
Arguments:
- layer_input: bfloat16 [4, 4096, 4096], P('dp', 'seq', 'head'), may hold values from -24 to 24
- head_input: bfloat16 [4, 4096, 4096], P('dp', 'seq', 'head'), may hold values from -6 to 6
- in_matrix: bfloat16 [4, 4096, 512], P('dp', 'seq', 'head'), may hold values from -6 to 6
- out_matrix: bfloat16 [4, 4096, 512], P('dp', 'seq', 'head'), may hold values from -6 to 6
- grad_output: bfloat16 [4, 4096, 4096], P('dp', 'seq', 'head'), may hold values from -0.59765625 to 0.59765625
- step_weight: bfloat16 [4096, 64], P(None, 'head'), may hold values from -0.09375 to 0.09375
- step_bias: float32 [64], P('head'), may hold values from -7 to -6
- decay_log: float32 [64], P('head'), may hold values from -6.22 to 2.78
Outputs:
- grad_heads: bfloat16 [4, 4096, 4096], P('dp', 'seq', 'head')
- grad_in_matrix: bfloat16 [4, 4096, 512], P('dp', 'seq', 'head')
- grad_out_matrix: bfloat16 [4, 4096, 512], P('dp', 'seq', 'head')
- grad_layer_input: bfloat16 [4, 4096, 4096], P('dp', 'seq', 'head')
- grad_step_weight: float32 [4096, 64], P(('seq', 'dp'), 'head')
The draws below stay inside these ranges and needn't reach their ends.
All inputs are finite; a program needn't handle non-finite values.
Results may differ from the reference program's by a relative error of at most 0.02.
Values may be sent and summed in bfloat16 or wider, within the bound.
No kernel may reach another device: no remote copies, remote signals or barrier semaphores. Data moves between devices by JAX's collectives and lax.ppermute only.
A program may use at most 64 MiB of HBM per device.

```python
import math
import jax
import jax.numpy as jnp
from jax import lax

D = 4096
H = 64
P_SIZE = 64
NSTATE = 128
G = 4
BLOCK = 128
TOK_DEV = 128
BATCH = 4
LEN = 4096
N_HEAD = 4


def draw_layer_input(key, part):
    first_key, second_key, third_key = jax.random.split(key, 3)
    base = jnp.clip(jax.random.normal(first_key, (BATCH, LEN, D), jnp.float32), -5.0, 5.0)
    block_count = LEN // TOK_DEV
    scales = jnp.exp(jax.random.uniform(second_key, (BATCH, block_count), jnp.float32, math.log(0.6), math.log(1.6)))
    row_scale = jnp.repeat(scales, TOK_DEV, axis=1)
    spots = jax.random.randint(third_key, (BATCH, 6), 0, LEN)
    positions = jnp.arange(LEN)
    struck = jnp.any(positions[None, :, None] == spots[:, None, :], axis=2)
    factor = jnp.where(struck, 3.0, 1.0)
    return (base * (row_scale * factor)[..., None]).astype(jnp.bfloat16)


def draw_decay_log(key, part):
    values = jax.random.uniform(key, (H,), jnp.float32, math.log(0.002), math.log(16.0))
    return values.astype(jnp.float32)


def block_levels(key, extent, cuts, low, high):
    def one(axis_at, parts):
        heights = jax.random.uniform(jax.random.fold_in(jax.random.fold_in(key, 6), axis_at), (parts,), jnp.float32, low / len(cuts), high / len(cuts))
        return jnp.repeat(jnp.exp(heights), extent[axis_at] // parts).reshape((-1,) + (1,) * (len(extent) - axis_at - 1))

    loudness = one(*cuts[0])
    for cut in cuts[1:]:
        loudness = loudness * one(*cut)
    return loudness


def bell_draw(own_key, shape, spread, reach, pieces=(), held_as=jnp.bfloat16):
    array = spread * jax.random.normal(own_key, shape, jnp.float32)
    if pieces:
        array = array * block_levels(own_key, shape, pieces, -0.22, 0.18)
    return jnp.clip(array, -reach, reach).astype(held_as)


def setup_inputs(seed: int = 0) -> dict:
    seeds = jax.random.split(jax.random.key(seed), 9)
    layer_input = draw_layer_input(jax.random.fold_in(seeds[8], 71), 0)
    head_input = bell_draw(seeds[1], (BATCH, LEN, H * P_SIZE), 1.0, 6.0, ((0, 4), (1, 32), (2, 4)))
    in_matrix = bell_draw(seeds[2], (BATCH, LEN, G * NSTATE), 1.0, 6.0, ((0, 4), (1, 32), (2, 4)))
    out_matrix = bell_draw(seeds[3], (BATCH, LEN, G * NSTATE), 1.0, 6.0, ((0, 4), (1, 32), (2, 4)))
    grad_output = bell_draw(seeds[4], (BATCH, LEN, H * P_SIZE), 0.1, 0.59765625, ((0, 4), (1, 32), (2, 4)))
    step_weight = bell_draw(seeds[5], (D, H), D ** -0.5, 0.09375, ((1, 4),))
    step_bias = jnp.clip(-7.0 + 1.0 * jax.random.uniform(seeds[6], (H,), jnp.float32) ** block_levels(seeds[6], (H,), ((0, 4),), -0.2, 0.2), -7.0, -6.0)
    decay_log = draw_decay_log(jax.random.fold_in(seeds[8], 71), 0)
    return {"layer_input": layer_input, "head_input": head_input, "in_matrix": in_matrix, "out_matrix": out_matrix, "grad_output": grad_output, "step_weight": step_weight, "step_bias": step_bias, "decay_log": decay_log}


PRECISION_LEVEL = lax.Precision.HIGHEST

def block_step(carry_state, inputs):
    input_block, b_block, c_block, step_block, decay_block = inputs
    cumulated = jnp.cumsum(decay_block, axis=-1)
    block_len = cumulated.shape[-1]
    lower_mask = jnp.arange(block_len)[:, None] >= jnp.arange(block_len)[None, :]
    decay_span = jnp.exp(jnp.where(lower_mask, cumulated[..., :, None] - cumulated[..., None, :], -1e+30))
    kernel = jnp.einsum('tgn,sgn->gts', c_block, b_block, precision=PRECISION_LEVEL)
    weight_values = kernel[:, None] * decay_span * step_block[..., None, :]
    within_block = jnp.einsum('idwz,zidx->widx', weight_values, input_block, precision=PRECISION_LEVEL)
    carried = jnp.einsum('tgn,grnp->tgrp', c_block, carry_state, precision=PRECISION_LEVEL)
    output = within_block + jnp.moveaxis(jnp.exp(cumulated), -1, 0)[..., None] * carried
    totals = cumulated[..., -1]
    inflow = jnp.exp(totals[..., None] - cumulated) * step_block
    fresh_term = jnp.einsum('grs,sgn,sgrp->grnp', inflow, b_block, input_block, precision=PRECISION_LEVEL)
    return (jnp.exp(totals)[..., None, None] * carry_state + fresh_term, output)

def segment(x_rows, b_rows, readout_rows, step_sizes, decays, start_state):
    length = x_rows.shape[0]
    blocks = length // BLOCK

    def split_rows(values):
        return values.reshape((blocks, BLOCK) + values.shape[1:])

    def split_last(values):
        return jnp.moveaxis(values.reshape(values.shape[:-1] + (blocks, BLOCK)), -2, 0)
    final_state, outputs = lax.scan(block_step, start_state, (split_rows(x_rows), split_rows(b_rows), split_rows(readout_rows), split_last(step_sizes), split_last(decays)))
    return (outputs.reshape(x_rows.shape), final_state)

def reference(layer_input, head_input, in_matrix, out_matrix, grad_output, step_weight, step_bias, decay_log):
    ratio = H // G
    rates = jnp.exp(decay_log).reshape(G, ratio)
    heads_per_shard = H // N_HEAD

    def one_sequence(items):
        seq_input, seq_heads, seq_in, seq_out, seq_grad = items
        preact = jnp.dot(seq_input, step_weight, preferred_element_type=jnp.float32) + step_bias
        step_sizes = jnp.transpose(jax.nn.softplus(preact)).reshape(G, ratio, LEN)
        x_rows = seq_heads.astype(jnp.float32).reshape(LEN, G, ratio, P_SIZE)
        b_rows = seq_in.astype(jnp.float32).reshape(LEN, G, NSTATE)
        readout_rows = seq_out.astype(jnp.float32).reshape(LEN, G, NSTATE)
        output_gradient = seq_grad.astype(jnp.float32).reshape(LEN, G, ratio, P_SIZE)
        start_state = jnp.zeros((G, ratio, NSTATE, P_SIZE), jnp.float32)

        def forward(x_arg, b_arg, c_arg, step_arg):
            return segment(x_arg, b_arg, c_arg, step_arg, -rates[..., None] * step_arg, start_state)[0]
        forward_out, pullback = jax.vjp(forward, x_rows, b_rows, readout_rows, step_sizes)
        grad_x, grad_b, grad_c, grad_step = pullback(output_gradient)
        grad_pre = (jnp.transpose(grad_step.reshape(H, LEN)) * jax.nn.sigmoid(preact)).astype(jnp.bfloat16)
        grad_input = jnp.zeros((LEN, D), jnp.float32)
        for shard_index in range(N_HEAD):
            first = shard_index * heads_per_shard
            partial_value = lax.dot_general(grad_pre[:, first:first + heads_per_shard], step_weight[:, first:first + heads_per_shard], (((1,), (1,)), ((), ())), preferred_element_type=jnp.float32)
            grad_input = grad_input + lax.optimization_barrier(partial_value.astype(jnp.bfloat16)).astype(jnp.float32)
        grad_weight = lax.dot_general(seq_input, grad_pre, (((0,), (0,)), ((), ())), preferred_element_type=jnp.float32)
        return (grad_x.reshape(LEN, H * P_SIZE).astype(jnp.bfloat16), grad_b.reshape(LEN, G * NSTATE).astype(jnp.bfloat16), grad_c.reshape(LEN, G * NSTATE).astype(jnp.bfloat16), grad_input.astype(jnp.bfloat16), grad_weight)
    results = lax.map(one_sequence, (layer_input, head_input, in_matrix, out_matrix, grad_output))
    return (results[0], results[1], results[2], results[3], lax.optimization_barrier(jnp.sum(results[4], axis=0)))
```

```python
import jax
import jax.numpy as jnp
from jax import lax
from jax.experimental import pallas as pl
from jax.experimental.pallas import tpu as pltpu
from jax.sharding import PartitionSpec as P

P_SIZE = 64
NSTATE = 128
LANES = 128
EXTRA = 8
F32 = jnp.float32
BF16 = jnp.bfloat16
EXACT = lax.Precision.HIGHEST


def dot(a, b, ca, cb, precision=None):
    return lax.dot_general(
        a, b, (((ca,), (cb,)), ((), ())), preferred_element_type=F32, precision=precision
    )


def iota(shape, axis):
    return lax.broadcasted_iota(jnp.int32, shape, axis)


def halves(value):
    high = value.astype(BF16)
    return high, (value - high.astype(F32)).astype(BF16)


def segment_matrix(heads):
    shape = (heads, heads * P_SIZE)
    first = iota(shape, 0) * P_SIZE
    lane = iota(shape, 1)
    inside = jnp.logical_and(lane >= first, lane < first + P_SIZE)
    return jnp.where(inside, 1.0, 0.0).astype(BF16)


def expand(value, segments):
    high, low = halves(jnp.transpose(value))
    return dot(high, segments, 1, 0) + dot(low, segments, 1, 0)


def gather_heads(value, segments):
    high, low = halves(value)
    return dot(segments, high, 1, 1) + dot(segments, low, 1, 1)


def column(row):
    size = row.shape[1]
    diagonal = iota((size, size), 0) == iota((size, size), 1)
    return jnp.sum(jnp.where(diagonal, row, 0.0), axis=1, keepdims=True)


def pack_kernel(input_ref, weight_ref, out_ref):
    parts, _, width = out_ref.shape
    tokens = input_ref.shape[0]
    for part in range(parts):
        out_ref[part, :tokens, :] = input_ref[...]
        out_ref[part, tokens:, :] = weight_ref[:, part * width : (part + 1) * width]


def spread(shrink, states_ref, heads):
    slices, rows, _ = states_ref.shape
    first = shrink.astype(BF16).astype(F32)
    second = (shrink - first).astype(BF16).astype(F32)
    third = shrink - first - second
    place = iota((EXTRA, NSTATE), 0)
    each = slices // heads
    for head in range(heads):
        one = slice(head, head + 1)
        tile = jnp.where(place == 0, first[one], jnp.where(place == 1, second[one], third[one]))
        tile = jnp.where(place < 3, tile, 0.0).astype(BF16)
        for index in range(head * each, (head + 1) * each):
            states_ref[index, rows - EXTRA :, :] = tile


def state_kernel(
    whole_ref, weight_ref, bias_ref, log_ref, x_ref, b_ref, c_ref, g_ref,
    states_ref, small_ref, xs_ref, gs_ref,
):
    parts, _, width = whole_ref.shape
    heads = weight_ref.shape[0]
    tokens = x_ref.shape[0]
    slices = states_ref.shape[0]
    rows = heads * P_SIZE // slices
    preact = column(bias_ref[...])
    for part in range(parts):
        preact = preact + dot(
            weight_ref[:, part * width : (part + 1) * width], whole_ref[part, :tokens, :], 1, 1
        )
    tail = jnp.exp(-jnp.abs(preact))
    step = jnp.maximum(preact, 0.0) + jnp.log1p(tail)
    rate = jnp.exp(column(log_ref[...]))
    upto = jnp.where(iota((tokens, tokens), 0) <= iota((tokens, tokens), 1), 1.0, 0.0)
    cumulated = dot(-rate * step, upto, 1, 0, EXACT)
    total = cumulated[:, tokens - 1 :]
    small_ref[0] = preact
    small_ref[1] = step
    small_ref[2] = cumulated
    inflow = jnp.exp(total - cumulated) * step
    segments = segment_matrix(heads)
    scaled = (x_ref[...].astype(F32) * expand(inflow, segments)).astype(BF16)
    xs_ref[...] = scaled
    state = dot(scaled, b_ref[...], 0, 0).astype(BF16)
    states_ref[:, :rows, :] = state.reshape(slices, rows, NSTATE)
    scaled = (g_ref[...].astype(F32) * expand(jnp.exp(cumulated), segments)).astype(BF16)
    gs_ref[...] = scaled
    grad = dot(scaled, c_ref[...], 0, 0).astype(BF16)
    states_ref[:, rows : 2 * rows, :] = grad.reshape(slices, rows, NSTATE)
    spread(jnp.exp(total), states_ref, heads)


def scan_kernel(states_ref, out_ref):
    count, rows2, _ = out_ref.shape
    rows = rows2 // 2
    shrink = [
        jnp.sum(states_ref[place, rows2:, :].astype(F32), axis=0, keepdims=True)
        for place in range(count)
    ]
    for start, order in ((0, range(count)), (rows, reversed(range(count)))):
        state = jnp.zeros((rows, NSTATE), F32)
        for place in order:
            out_ref[place, start : start + rows, :] = state.astype(BF16)
            state = shrink[place] * state + states_ref[
                place, start : start + rows, :
            ].astype(F32)


def inner_kernel(small_ref, x_ref, b_ref, c_ref, g_ref, inner_ref, kernel_ref, sums_ref):
    _, heads, tokens = small_ref.shape
    cumulated = small_ref[2]
    kernel = dot(b_ref[...], c_ref[...], 1, 1)
    step_column = jnp.transpose(small_ref[1])
    cumulated_column = jnp.transpose(cumulated)
    allowed = iota((tokens, tokens), 0) <= iota((tokens, tokens), 1)
    lower = iota((tokens, LANES), 1) < P_SIZE
    zero = jnp.zeros((tokens, LANES), BF16)
    d_kernel = jnp.zeros((tokens, tokens), F32)
    row_sums = []
    products = []
    for pair in range(heads // 2):
        lanes = slice(pair * LANES, (pair + 1) * LANES)
        x = x_ref[:, lanes]
        g = g_ref[:, lanes]
        both = []
        for half in range(2):
            head = 2 * pair + half
            span = cumulated[head : head + 1, :] - cumulated_column[:, head : head + 1]
            span = jnp.exp(jnp.where(allowed, span, -1e30))
            mine = jnp.where(lower, x, zero) if half == 0 else jnp.where(lower, zero, x)
            product = dot(mine, g, 1, 1) * span * step_column[:, head : head + 1]
            d_kernel = d_kernel + product
            row_sums.append(jnp.sum(product * kernel, axis=0, keepdims=True))
            both.append(dot((span * kernel).astype(BF16), g, 1, 0))
        inner = jnp.where(lower, both[0], both[1])
        inner_ref[:, lanes] = inner
        products.append(x.astype(F32) * inner)
    kernel_ref[...] = d_kernel.astype(BF16)
    sums_ref[0] = jnp.concatenate(row_sums, axis=0)
    sums_ref[1] = gather_heads(jnp.concatenate(products, axis=1), segment_matrix(heads))


def last_kernel(
    states_ref, small_ref, log_ref, inner_ref, kernel_ref, sums_ref,
    x_ref, b_ref, c_ref, g_ref, xs_ref, gs_ref, whole_ref,
    gx_ref, gb_ref, gc_ref, pre_ref, part_ref,
):
    _, heads, tokens = small_ref.shape
    preact = small_ref[0]
    step = small_ref[1]
    cumulated = small_ref[2]
    total = cumulated[:, tokens - 1 :]
    rate = jnp.exp(column(log_ref[...]))
    left = jnp.exp(total - cumulated)
    segments = segment_matrix(heads)
    rows = states_ref.shape[1] // 2
    state = states_ref[:, :rows, :].reshape(heads * P_SIZE, NSTATE)
    grad = states_ref[:, rows:, :].reshape(heads * P_SIZE, NSTATE)
    x = x_ref[...].astype(F32)
    from_grad = dot(b_ref[...], grad, 1, 1)
    from_state = dot(c_ref[...], state, 1, 1)
    readout = jnp.exp(cumulated) * gather_heads(g_ref[...].astype(F32) * from_state, segments)
    gx_ref[...] = (
        expand(step, segments) * (inner_ref[...] + expand(left, segments) * from_grad)
    ).astype(BF16)
    inflow_part = left * gather_heads(x * from_grad, segments)
    direct = sums_ref[1] + inflow_part
    high, low = halves(state.astype(F32) * grad.astype(F32))
    meeting = jnp.sum(dot(segments, high, 1, 0) + dot(segments, low, 1, 0), axis=1, keepdims=True)
    of_total = jnp.sum(step * inflow_part, axis=1, keepdims=True) + jnp.exp(total) * meeting
    of_cumulated = sums_ref[0] + readout - step * direct
    onward = jnp.where(iota((tokens, tokens), 0) >= iota((tokens, tokens), 1), 1.0, 0.0)
    of_decay = dot(of_cumulated, onward, 1, 0, EXACT) + of_total
    grad_step = direct - rate * of_decay
    sigmoid = 1.0 / (1.0 + jnp.exp(-preact))
    grad_pre = (grad_step * sigmoid).astype(BF16)
    gb_ref[...] = (
        dot(kernel_ref[...], c_ref[...], 1, 0) + dot(xs_ref[...], grad, 1, 0)
    ).astype(BF16)
    gc_ref[...] = (
        dot(kernel_ref[...], b_ref[...], 0, 0) + dot(gs_ref[...], state, 1, 0)
    ).astype(BF16)
    pre_ref[...] = grad_pre
    per = part_ref.shape[1]
    shards = heads // per
    size = LANES // shards
    shape = (heads, heads)
    swapped = iota(shape, 1) == shards * (iota(shape, 0) % per) + iota(shape, 0) // per
    swapped = dot(jnp.where(swapped, 1.0, 0.0).astype(BF16), grad_pre, 1, 0).astype(BF16)
    group = 8 // per
    block = iota((8, LANES), 1) // size
    row = iota((8, LANES), 0) // per
    masks = [
        jnp.logical_and(block == index, row == index % group) for index in range(shards)
    ]
    parts, _, width = whole_ref.shape
    for part in range(parts):
        term = dot(swapped, whole_ref[part, :tokens, :], 1, 0)
        for index in range(width // LANES):
            lanes = slice(index * LANES, (index + 1) * LANES)
            turned = []
            for first in range(0, heads, 8):
                piece = term[first : first + 8, lanes]
                turned.append(
                    [piece] + [pltpu.roll(piece, size * turn, 1) for turn in range(1, shards)]
                )
            for shard in range(shards):
                packed = jnp.zeros((8, LANES), F32)
                for index2 in range(shards):
                    source = turned[index2 // group][(index2 - shard) % shards]
                    packed = jnp.where(masks[index2], source, packed)
                total_rows = packed[:per]
                for other in range(1, group):
                    total_rows = total_rows + packed[other * per : (other + 1) * per]
                where = (part * (width // LANES) + index) * shards + shard
                part_ref[where] = total_rows.astype(part_ref.dtype)


def input_kernel(place_ref, whole_ref, *refs):
    out_ref = refs[-1]
    parts = whole_ref.shape[0]
    tokens = out_ref.shape[0]
    pre = jnp.concatenate([ref[...] for ref in refs[:-1]], axis=0)
    weight = jnp.concatenate(
        [whole_ref[lax.rem(place_ref[0] + parts - shift, parts), tokens:, :] for shift in range(parts)],
        axis=0,
    )
    out_ref[...] = dot(pre, weight, 0, 0).astype(BF16)


def sum_kernel(part_ref, out_ref):
    heads, size = out_ref.shape
    total = jnp.sum(part_ref[...].astype(F32), axis=0)
    per = total.shape[0]
    shards = heads // per
    for shard in range(shards):
        piece = total[:, shard * size : (shard + 1) * size]
        for row in range(per):
            head = row * shards + shard
            out_ref[head : head + 1, :] = piece[row : row + 1, :]


def call(kernel, out_shape, *args, micros=2, scalars=0):
    cost = pl.CostEstimate(flops=0, transcendentals=0, bytes_accessed=micros * 3_000_000)
    specs = [pl.BlockSpec(memory_space=pltpu.SMEM)] * scalars
    specs += [pl.BlockSpec(memory_space=pltpu.VMEM)] * (len(args) - scalars)
    return pl.pallas_call(
        kernel, out_shape=out_shape, in_specs=specs, name=kernel.__name__, cost_estimate=cost
    )(*args)


def exchange(value, axis):
    return lax.all_to_all(value, axis, 0, 0, tiled=True)


def body(
    layer_input, head_input, in_matrix, out_matrix, grad_output, step_weight, step_bias, decay_log
):
    parts = lax.axis_size("head")
    places = lax.axis_size("seq")
    shards = lax.axis_size("dp")
    tokens, width = layer_input.shape[1:]
    heads = step_weight.shape[1]
    rows = heads * P_SIZE // places
    shape = jax.ShapeDtypeStruct
    x, b, c, g = head_input[0], in_matrix[0], out_matrix[0], grad_output[0]
    weight = step_weight.T
    bias = step_bias.reshape(1, heads)
    logs = decay_log.reshape(1, heads)
    packed = call(
        pack_kernel, shape((parts, tokens + heads, width), BF16), layer_input[0], weight
    )
    whole = exchange(packed, "head")
    states, small, xs, gs = call(
        state_kernel,
        (
            shape((places, 2 * rows + EXTRA, NSTATE), BF16),
            shape((3, heads, tokens), F32),
            shape(x.shape, BF16),
            shape(x.shape, BF16),
        ),
        whole, weight, bias, logs, x, b, c, g,
    )
    states = exchange(states, "seq")
    inner, kernel, sums = call(
        inner_kernel,
        (shape(x.shape, F32), shape((tokens, tokens), BF16), shape((2, heads, tokens), F32)),
        small, x, b, c, g,
    )
    states = call(scan_kernel, shape((places, 2 * rows, NSTATE), BF16), states)
    states = exchange(states, "seq")
    grad_x, grad_b, grad_c, pre, part = call(
        last_kernel,
        (
            shape(x.shape, BF16),
            shape(b.shape, BF16),
            shape(c.shape, BF16),
            shape((heads, tokens), BF16),
            shape((places * shards, heads // shards, LANES), BF16),
        ),
        states, small, logs, inner, kernel, sums, x, b, c, g, xs, gs, whole,
    )
    part = exchange(part, ("seq", "dp"))
    others = [
        lax.ppermute(pre, "head", [(i, (i + shift) % parts) for i in range(parts)])
        for shift in range(1, parts)
    ]
    place = lax.axis_index("head").astype(jnp.int32).reshape(1)
    grad_input = call(
        input_kernel, shape((tokens, width), BF16), place, whole, pre, *others, scalars=1
    )
    term = call(sum_kernel, shape((heads, LANES // shards), F32), part)
    return (grad_x[None], grad_b[None], grad_c[None], grad_input[None], term.T)


def solution(mesh):
    in_specs = (P("dp", "seq", "head"),) * 5 + (P(None, "head"), P("head"), P("head"))
    out_specs = (P("dp", "seq", "head"),) * 4 + (P(("seq", "dp"), "head"),)
    return jax.shard_map(body, mesh=mesh, in_specs=in_specs, out_specs=out_specs, check_vma=False)
```

```python
import jax
import jax.numpy as jnp
from jax import lax
from jax.experimental import pallas as pl
from jax.experimental.pallas import tpu as pltpu
from jax.sharding import PartitionSpec as P

P_SIZE = 64
NSTATE = 128
LANES = 128
EXTRA = 8
F32 = jnp.float32
BF16 = jnp.bfloat16
EXACT = lax.Precision.HIGHEST


def dot(a, b, ca, cb, precision=None):
    return lax.dot_general(
        a, b, (((ca,), (cb,)), ((), ())), preferred_element_type=F32, precision=precision
    )


def iota(shape, axis):
    return lax.broadcasted_iota(jnp.int32, shape, axis)


def halves(value):
    high = value.astype(BF16)
    return high, (value - high.astype(F32)).astype(BF16)


def segment_matrix(heads):
    shape = (heads, heads * P_SIZE)
    first = iota(shape, 0) * P_SIZE
    lane = iota(shape, 1)
    inside = jnp.logical_and(lane >= first, lane < first + P_SIZE)
    return jnp.where(inside, 1.0, 0.0).astype(BF16)


def expand(value, segments):
    high, low = halves(jnp.transpose(value))
    return dot(high, segments, 1, 0) + dot(low, segments, 1, 0)


def gather_heads(value, segments):
    high, low = halves(value)
    return dot(segments, high, 1, 1) + dot(segments, low, 1, 1)


def column(row):
    size = row.shape[1]
    diagonal = iota((size, size), 0) == iota((size, size), 1)
    return jnp.sum(jnp.where(diagonal, row, 0.0), axis=1, keepdims=True)


def pack_kernel(input_ref, weight_ref, out_ref):
    parts, _, width = out_ref.shape
    tokens = input_ref.shape[0]
    for part in range(parts):
        out_ref[part, :tokens, :] = input_ref[...]
        out_ref[part, tokens:, :] = weight_ref[:, part * width : (part + 1) * width]


def spread(shrink, states_ref, heads):
    slices, rows, _ = states_ref.shape
    first = shrink.astype(BF16).astype(F32)
    second = (shrink - first).astype(BF16).astype(F32)
    third = shrink - first - second
    place = iota((EXTRA, NSTATE), 0)
    each = slices // heads
    for head in range(heads):
        one = slice(head, head + 1)
        tile = jnp.where(place == 0, first[one], jnp.where(place == 1, second[one], third[one]))
        tile = jnp.where(place < 3, tile, 0.0).astype(BF16)
        for index in range(head * each, (head + 1) * each):
            states_ref[index, rows - EXTRA :, :] = tile


def state_kernel(
    whole_ref, weight_ref, bias_ref, log_ref, x_ref, b_ref, c_ref, g_ref,
    states_ref, small_ref, xs_ref, gs_ref,
):
    parts, _, width = whole_ref.shape
    heads = weight_ref.shape[0]
    tokens = x_ref.shape[0]
    slices = states_ref.shape[0]
    rows = heads * P_SIZE // slices
    preact = column(bias_ref[...])
    for part in range(parts):
        preact = preact + dot(
            weight_ref[:, part * width : (part + 1) * width], whole_ref[part, :tokens, :], 1, 1
        )
    tail = jnp.exp(-jnp.abs(preact))
    step = jnp.maximum(preact, 0.0) + jnp.log1p(tail)
    rate = jnp.exp(column(log_ref[...]))
    upto = jnp.where(iota((tokens, tokens), 0) <= iota((tokens, tokens), 1), 1.0, 0.0)
    cumulated = dot(-rate * step, upto, 1, 0, EXACT)
    total = cumulated[:, tokens - 1 :]
    small_ref[0] = preact
    small_ref[1] = step
    small_ref[2] = cumulated
    inflow = jnp.exp(total - cumulated) * step
    segments = segment_matrix(heads)
    scaled = (x_ref[...].astype(F32) * expand(inflow, segments)).astype(BF16)
    xs_ref[...] = scaled
    state = dot(scaled, b_ref[...], 0, 0).astype(BF16)
    states_ref[:, :rows, :] = state.reshape(slices, rows, NSTATE)
    scaled = (g_ref[...].astype(F32) * expand(jnp.exp(cumulated), segments)).astype(BF16)
    gs_ref[...] = scaled
    grad = dot(scaled, c_ref[...], 0, 0).astype(BF16)
    states_ref[:, rows : 2 * rows, :] = grad.reshape(slices, rows, NSTATE)
    spread(jnp.exp(total), states_ref, heads)


def scan_kernel(states_ref, out_ref):
    count, rows2, _ = out_ref.shape
    rows = rows2 // 2
    shrink = [
        jnp.sum(states_ref[place, rows2:, :].astype(F32), axis=0, keepdims=True)
        for place in range(count)
    ]
    for start, order in ((0, range(count)), (rows, reversed(range(count)))):
        state = jnp.zeros((rows, NSTATE), F32)
        for place in order:
            out_ref[place, start : start + rows, :] = state.astype(BF16)
            state = shrink[place] * state + states_ref[
                place, start : start + rows, :
            ].astype(F32)


def inner_kernel(small_ref, x_ref, b_ref, c_ref, g_ref, inner_ref, kernel_ref, sums_ref):
    _, heads, tokens = small_ref.shape
    cumulated = small_ref[2]
    kernel = dot(b_ref[...], c_ref[...], 1, 1)
    step_column = jnp.transpose(small_ref[1])
    cumulated_column = jnp.transpose(cumulated)
    allowed = iota((tokens, tokens), 0) <= iota((tokens, tokens), 1)
    lower = iota((tokens, LANES), 1) < P_SIZE
    zero = jnp.zeros((tokens, LANES), BF16)
    d_kernel = jnp.zeros((tokens, tokens), F32)
    row_sums = []
    products = []
    for pair in range(heads // 2):
        lanes = slice(pair * LANES, (pair + 1) * LANES)
        x = x_ref[:, lanes]
        g = g_ref[:, lanes]
        both = []
        for half in range(2):
            head = 2 * pair + half
            span = cumulated[head : head + 1, :] - cumulated_column[:, head : head + 1]
            span = jnp.exp(jnp.where(allowed, span, -1e30))
            mine = jnp.where(lower, x, zero) if half == 0 else jnp.where(lower, zero, x)
            product = dot(mine, g, 1, 1) * span * step_column[:, head : head + 1]
            d_kernel = d_kernel + product
            row_sums.append(jnp.sum(product * kernel, axis=0, keepdims=True))
            both.append(dot((span * kernel).astype(BF16), g, 1, 0))
        inner = jnp.where(lower, both[0], both[1])
        inner_ref[:, lanes] = inner
        products.append(x.astype(F32) * inner)
    kernel_ref[...] = d_kernel.astype(BF16)
    sums_ref[0] = jnp.concatenate(row_sums, axis=0)
    sums_ref[1] = gather_heads(jnp.concatenate(products, axis=1), segment_matrix(heads))


def last_kernel(
    states_ref, small_ref, log_ref, inner_ref, kernel_ref, sums_ref,
    x_ref, b_ref, c_ref, g_ref, xs_ref, gs_ref, whole_ref,
    gx_ref, gb_ref, gc_ref, pre_ref, part_ref,
):
    _, heads, tokens = small_ref.shape
    preact = small_ref[0]
    step = small_ref[1]
    cumulated = small_ref[2]
    total = cumulated[:, tokens - 1 :]
    rate = jnp.exp(column(log_ref[...]))
    left = jnp.exp(total - cumulated)
    segments = segment_matrix(heads)
    rows = states_ref.shape[1] // 2
    state = states_ref[:, :rows, :].reshape(heads * P_SIZE, NSTATE)
    grad = states_ref[:, rows:, :].reshape(heads * P_SIZE, NSTATE)
    x = x_ref[...].astype(F32)
    from_grad = dot(b_ref[...], grad, 1, 1)
    from_state = dot(c_ref[...], state, 1, 1)
    readout = jnp.exp(cumulated) * gather_heads(g_ref[...].astype(F32) * from_state, segments)
    gx_ref[...] = (
        expand(step, segments) * (inner_ref[...] + expand(left, segments) * from_grad)
    ).astype(BF16)
    inflow_part = left * gather_heads(x * from_grad, segments)
    direct = sums_ref[1] + inflow_part
    high, low = halves(state.astype(F32) * grad.astype(F32))
    meeting = jnp.sum(dot(segments, high, 1, 0) + dot(segments, low, 1, 0), axis=1, keepdims=True)
    of_total = jnp.sum(step * inflow_part, axis=1, keepdims=True) + jnp.exp(total) * meeting
    of_cumulated = sums_ref[0] + readout - step * direct
    onward = jnp.where(iota((tokens, tokens), 0) >= iota((tokens, tokens), 1), 1.0, 0.0)
    of_decay = dot(of_cumulated, onward, 1, 0, EXACT) + of_total
    grad_step = direct - rate * of_decay
    sigmoid = 1.0 / (1.0 + jnp.exp(-preact))
    grad_pre = (grad_step * sigmoid).astype(BF16)
    gb_ref[...] = (
        dot(kernel_ref[...], c_ref[...], 1, 0) + dot(xs_ref[...], grad, 1, 0)
    ).astype(BF16)
    gc_ref[...] = (
        dot(kernel_ref[...], b_ref[...], 0, 0) + dot(gs_ref[...], state, 1, 0)
    ).astype(BF16)
    pre_ref[...] = grad_pre
    per = part_ref.shape[1]
    shards = heads // per
    size = LANES // shards
    shape = (heads, heads)
    swapped = iota(shape, 1) == shards * (iota(shape, 0) % per) + iota(shape, 0) // per
    swapped = dot(jnp.where(swapped, 1.0, 0.0).astype(BF16), grad_pre, 1, 0).astype(BF16)
    group = 8 // per
    block = iota((8, LANES), 1) // size
    row = iota((8, LANES), 0) // per
    masks = [
        jnp.logical_and(block == index, row == index % group) for index in range(shards)
    ]
    parts, _, width = whole_ref.shape
    for part in range(parts):
        term = dot(swapped, whole_ref[part, :tokens, :], 1, 0)
        for index in range(width // LANES):
            lanes = slice(index * LANES, (index + 1) * LANES)
            turned = []
            for first in range(0, heads, 8):
                piece = term[first : first + 8, lanes]
                turned.append(
                    [piece] + [pltpu.roll(piece, size * turn, 1) for turn in range(1, shards)]
                )
            for shard in range(shards):
                packed = jnp.zeros((8, LANES), F32)
                for index2 in range(shards):
                    source = turned[index2 // group][(index2 - shard) % shards]
                    packed = jnp.where(masks[index2], source, packed)
                total_rows = packed[:per]
                for other in range(1, group):
                    total_rows = total_rows + packed[other * per : (other + 1) * per]
                where = (part * (width // LANES) + index) * shards + shard
                part_ref[where] = total_rows.astype(part_ref.dtype)


def input_kernel(place_ref, whole_ref, *refs):
    out_ref = refs[-1]
    parts = whole_ref.shape[0]
    tokens = out_ref.shape[0]
    pre = jnp.concatenate([ref[...] for ref in refs[:-1]], axis=0)
    weight = jnp.concatenate(
        [whole_ref[lax.rem(place_ref[0] + parts - shift, parts), tokens:, :] for shift in range(parts)],
        axis=0,
    )
    out_ref[...] = dot(pre, weight, 0, 0).astype(BF16)


def sum_kernel(part_ref, out_ref):
    heads, size = out_ref.shape
    total = jnp.sum(part_ref[...].astype(F32), axis=0)
    per = total.shape[0]
    shards = heads // per
    for shard in range(shards):
        piece = total[:, shard * size : (shard + 1) * size]
        for row in range(per):
            head = row * shards + shard
            out_ref[head : head + 1, :] = piece[row : row + 1, :]


def inside(value):
    return pltpu.with_memory_space_constraint(value, pltpu.VMEM)


def call(kernel, out_shape, *args, micros=2, scalars=0):
    cost = pl.CostEstimate(flops=0, transcendentals=0, bytes_accessed=micros * 3_000_000)
    specs = [pl.BlockSpec(memory_space=pltpu.SMEM)] * scalars
    specs += [pl.BlockSpec(memory_space=pltpu.VMEM)] * (len(args) - scalars)
    return pl.pallas_call(
        kernel, out_shape=out_shape, in_specs=specs, name=kernel.__name__, cost_estimate=cost,
        compiler_params=pltpu.CompilerParams(vmem_limit_bytes=32 * 2**20),
    )(*args)


def exchange(value, axis):
    return inside(lax.all_to_all(value, axis, 0, 0, tiled=True))


def body(
    layer_input, head_input, in_matrix, out_matrix, grad_output, step_weight, step_bias, decay_log
):
    parts = lax.axis_size("head")
    places = lax.axis_size("seq")
    shards = lax.axis_size("dp")
    tokens, width = layer_input.shape[1:]
    heads = step_weight.shape[1]
    rows = heads * P_SIZE // places
    shape = jax.ShapeDtypeStruct
    near = pltpu.VMEM
    x, b, c, g = head_input[0], in_matrix[0], out_matrix[0], grad_output[0]
    weight = step_weight.T
    bias = step_bias.reshape(1, heads)
    logs = decay_log.reshape(1, heads)
    packed = call(
        pack_kernel, near((parts, tokens + heads, width), BF16), layer_input[0], weight
    )
    whole = exchange(packed, "head")
    states, small, xs, gs = call(
        state_kernel,
        (
            near((places, 2 * rows + EXTRA, NSTATE), BF16),
            near((3, heads, tokens), F32),
            near(x.shape, BF16),
            near(x.shape, BF16),
        ),
        whole, weight, bias, logs, x, b, c, g,
    )
    states = exchange(states, "seq")
    inner, kernel, sums = call(
        inner_kernel,
        (near(x.shape, F32), near((tokens, tokens), BF16), near((2, heads, tokens), F32)),
        small, x, b, c, g,
    )
    states = call(scan_kernel, near((places, 2 * rows, NSTATE), BF16), states)
    states = exchange(states, "seq")
    grad_x, grad_b, grad_c, pre, part = call(
        last_kernel,
        (
            shape(x.shape, BF16),
            shape(b.shape, BF16),
            shape(c.shape, BF16),
            near((heads, tokens), BF16),
            near((places * shards, heads // shards, LANES), BF16),
        ),
        states, small, logs, inner, kernel, sums, x, b, c, g, xs, gs, whole,
    )
    part = exchange(part, ("seq", "dp"))
    others = [
        inside(lax.ppermute(pre, "head", [(i, (i + shift) % parts) for i in range(parts)]))
        for shift in range(1, parts)
    ]
    place = lax.axis_index("head").astype(jnp.int32).reshape(1)
    grad_input = call(
        input_kernel, shape((tokens, width), BF16), place, whole, pre, *others, scalars=1
    )
    term = call(sum_kernel, shape((heads, LANES // shards), F32), part)
    return (grad_x[None], grad_b[None], grad_c[None], grad_input[None], term.T)


def solution(mesh):
    in_specs = (P("dp", "seq", "head"),) * 5 + (P(None, "head"), P("head"), P("head"))
    out_specs = (P("dp", "seq", "head"),) * 4 + (P(("seq", "dp"), "head"),)
    return jax.shard_map(body, mesh=mesh, in_specs=in_specs, out_specs=out_specs, check_vma=False)
```

```python
import jax
import jax.numpy as jnp
from jax import lax
from jax.experimental import pallas as pl
from jax.experimental.pallas import tpu as pltpu
from jax.sharding import PartitionSpec as P


P_SIZE = 64
NSTATE = 128
LANES = 128
NEAR = 4
EXTRA = 16
F32 = jnp.float32
BF16 = jnp.bfloat16
EXACT = lax.Precision.HIGHEST


def dot(a, b, ca, cb, precision=None):
    return lax.dot_general(
        a, b, (((ca,), (cb,)), ((), ())), preferred_element_type=F32, precision=precision
    )


def iota(shape, axis):
    return lax.broadcasted_iota(jnp.int32, shape, axis)


def halves(value):
    high = value.astype(BF16)
    return high, (value - high.astype(F32)).astype(BF16)


def thirds(value):
    first = value.astype(BF16).astype(F32)
    second = (value - first).astype(BF16).astype(F32)
    return first, second, value - first - second


def segment_matrix(rows, each, at):
    shape = (rows, each * P_SIZE)
    head = iota(shape, 0) - at * each
    lane = iota(shape, 1)
    inside = jnp.logical_and(lane >= head * P_SIZE, lane < head * P_SIZE + P_SIZE)
    return jnp.where(inside, 1.0, 0.0).astype(BF16)


def column(row, place, rows, each):
    size = row.shape[1]
    shape = (rows, size)
    mine = iota(shape, 1) == place * each + lax.rem(iota(shape, 0), each)
    return jnp.sum(jnp.where(mine, row, 0.0), axis=1, keepdims=True)


def spread(parts, segments):
    return dot(parts[0], segments, 1, 0) + dot(parts[1], segments, 1, 0)


def gathered(value, segments):
    high, low = halves(value)
    return dot(segments, high, 1, 1) + dot(segments, low, 1, 1)


def views(data_ref, at, wide):
    return (
        data_ref[at, :, :wide],
        data_ref[at, :, wide : 2 * wide],
        data_ref[at, :, 2 * wide : 2 * wide + NSTATE],
        data_ref[at, :, 2 * wide + NSTATE :],
    )


def pack_kernel(input_ref, weight_ref, out_ref):
    parts, _, width = out_ref.shape
    tokens = input_ref.shape[0]
    for part in range(parts):
        out_ref[part, :tokens, :] = input_ref[...]
        out_ref[part, tokens:, :] = weight_ref[:, part * width : (part + 1) * width]


def data_kernel(x_ref, g_ref, b_ref, c_ref, *out_refs):
    wide = x_ref.shape[1] // NEAR

    def fill(out_ref, quarter):
        lanes = slice(quarter * wide, (quarter + 1) * wide)
        out_ref[:, :wide] = x_ref[:, lanes]
        out_ref[:, wide : 2 * wide] = g_ref[:, lanes]

    for shift, out_ref in enumerate(out_refs):
        target = lax.rem(lax.rem(lax.axis_index("seq"), NEAR) + shift, NEAR)
        for quarter in range(NEAR):
            pl.when(target == quarter)(lambda o=out_ref, q=quarter: fill(o, q))
        out_ref[:, 2 * wide : 2 * wide + NSTATE] = b_ref[...]
        out_ref[:, 2 * wide + NSTATE :] = c_ref[...]


def preact_kernel(whole_ref, weight_ref, bias_ref, out_ref):
    parts, _, width = whole_ref.shape
    near, each, tokens = out_ref.shape
    term = column(bias_ref[...], 0, near * each, near * each)
    for part in range(parts):
        term = term + dot(
            weight_ref[:, part * width : (part + 1) * width], whole_ref[part, :tokens, :], 1, 1
        )
    out_ref[...] = term.reshape(near, each, tokens)


def state_kernel(terms_ref, log_ref, *refs):
    received = refs[:NEAR]
    sent_ref, data_ref, small_ref, states_ref, scaled_ref = refs[NEAR:]
    each, tokens = terms_ref.shape[1:]
    rows = NEAR * each
    wide = each * P_SIZE
    place = lax.rem(lax.axis_index("seq"), NEAR)
    for shift in range(NEAR):
        data_ref[lax.rem(place + NEAR - shift, NEAR)] = received[shift][...]
    preact = jnp.concatenate([terms_ref[at] for at in range(NEAR)], axis=0)
    tail = jnp.exp(-jnp.abs(preact))
    step = jnp.maximum(preact, 0.0) + jnp.log1p(tail)
    rate = jnp.exp(column(log_ref[...], place, rows, each))
    upto = jnp.where(iota((tokens, tokens), 0) <= iota((tokens, tokens), 1), 1.0, 0.0)
    cumulated = dot(-rate * step, upto, 1, 0, EXACT)
    total = cumulated[:, tokens - 1 :]
    small_ref[0] = preact
    small_ref[1] = step
    small_ref[2] = cumulated
    small_ref[3] = jnp.broadcast_to(rate, cumulated.shape)
    inflow = halves(jnp.transpose(jnp.exp(total - cumulated) * step))
    since = halves(jnp.transpose(jnp.exp(cumulated)))
    for at in range(NEAR):
        segments = segment_matrix(rows, each, at)
        x, g, b, c = views(data_ref, at, wide)
        scaled = (x.astype(F32) * spread(inflow, segments)).astype(BF16)
        scaled_ref[0, at] = scaled
        states_ref[0, at] = dot(scaled, b, 0, 0).astype(BF16)
        scaled = (g.astype(F32) * spread(since, segments)).astype(BF16)
        scaled_ref[1, at] = scaled
        states_ref[1, at] = dot(scaled, c, 0, 0).astype(BF16)
    shrink = jnp.exp(total)
    slices = sent_ref.shape[0]
    piece = wide // slices
    line = iota((EXTRA, NSTATE), 0)
    for head in range(each):
        lines = slice(head * P_SIZE, (head + 1) * P_SIZE)
        factor = [shrink[at * each + head : at * each + head + 1] for at in range(NEAR)]
        both = []
        for which, order in ((0, range(NEAR)), (1, reversed(range(NEAR)))):
            state = None
            for at in order:
                here = states_ref[which, at, lines, :].astype(F32)
                state = here if state is None else factor[at] * state + here
            both.append(state)
        whole = factor[0]
        for at in range(1, NEAR):
            whole = whole * factor[at]
        first, second, third = thirds(whole)
        tile = jnp.where(line == 0, first, jnp.where(line == 1, second, third))
        tile = jnp.where(line < 3, tile, 0.0).astype(BF16)
        for part in range(P_SIZE // piece):
            index = head * (P_SIZE // piece) + part
            for which in range(2):
                sent_ref[index, which * piece : (which + 1) * piece, :] = both[which][
                    part * piece : (part + 1) * piece
                ].astype(BF16)
            sent_ref[index, 2 * piece :, :] = tile


def far_kernel(states_ref, out_ref):
    count, rows2, _ = out_ref.shape
    rows = rows2 // 2
    shrink = [
        jnp.sum(states_ref[at, rows2 : rows2 + 3, :].astype(F32), axis=0, keepdims=True)
        for at in range(count)
    ]
    for start, order in ((0, range(count)), (rows, reversed(range(count)))):
        state = jnp.zeros((rows, NSTATE), F32)
        for at in order:
            out_ref[at, start : start + rows, :] = state.astype(BF16)
            state = shrink[at] * state + states_ref[at, start : start + rows, :].astype(F32)


def inner_kernel(data_ref, small_ref, inner_ref, pair_ref, sums_ref):
    _, rows, tokens = small_ref.shape
    each = rows // NEAR
    wide = each * P_SIZE
    cumulated = small_ref[2]
    step_column = jnp.transpose(small_ref[1])
    cumulated_column = jnp.transpose(cumulated)
    allowed = iota((tokens, tokens), 0) <= iota((tokens, tokens), 1)
    lower = iota((tokens, LANES), 1) < P_SIZE
    zero = jnp.zeros((tokens, LANES), BF16)
    row_sums = []
    direct = jnp.zeros((rows, tokens), F32)
    for at in range(NEAR):
        x_all, g_all, b, c = views(data_ref, at, wide)
        kernel = dot(b, c, 1, 1)
        d_kernel = jnp.zeros((tokens, tokens), F32)
        products = []
        for pair in range(each // 2):
            lanes = slice(pair * LANES, (pair + 1) * LANES)
            x = x_all[:, lanes]
            g = g_all[:, lanes]
            both = []
            for half in range(2):
                row = at * each + 2 * pair + half
                span = cumulated[row : row + 1, :] - cumulated_column[:, row : row + 1]
                span = jnp.exp(jnp.where(allowed, span, -1e30))
                mine = jnp.where(lower, x, zero) if half == 0 else jnp.where(lower, zero, x)
                product = dot(mine, g, 1, 1) * span * step_column[:, row : row + 1]
                d_kernel = d_kernel + product
                row_sums.append(jnp.sum(product * kernel, axis=0, keepdims=True))
                both.append(dot((span * kernel).astype(BF16), g, 1, 0))
            inner = jnp.where(lower, both[0], both[1])
            inner_ref[at, :, lanes] = inner.astype(BF16)
            products.append(x.astype(F32) * inner)
        d_kernel = d_kernel.astype(BF16)
        pair_ref[0, at] = dot(d_kernel, c, 1, 0).astype(BF16)
        pair_ref[1, at] = dot(d_kernel, b, 0, 0).astype(BF16)
        direct = direct + gathered(
            jnp.concatenate(products, axis=1), segment_matrix(rows, each, at)
        )
    sums_ref[0] = jnp.concatenate(row_sums, axis=0)
    sums_ref[1] = direct


def last_kernel(
    far_ref, data_ref, small_ref, states_ref, scaled_ref, inner_ref, pair_ref,
    sums_ref, *refs
):
    own_refs = refs[:NEAR]
    pre_ref, result_ref = refs[NEAR:]
    _, rows, tokens = small_ref.shape
    each = rows // NEAR
    wide = each * P_SIZE
    place = lax.rem(lax.axis_index("seq"), NEAR)
    preact = small_ref[0]
    step = small_ref[1]
    cumulated = small_ref[2]
    total = cumulated[:, tokens - 1 :]
    shrink = jnp.exp(total)
    rate = small_ref[3]
    left = jnp.exp(total - cumulated)
    piece = far_ref.shape[1] // 2

    def faded(state, at):
        return jnp.concatenate(
            [
                shrink[at * each + head : at * each + head + 1]
                * state[head * P_SIZE : (head + 1) * P_SIZE]
                for head in range(each)
            ],
            axis=0,
        )

    coming = [far_ref[:, :piece, :].reshape(wide, NSTATE).astype(F32)]
    for at in range(NEAR - 1):
        coming.append(faded(coming[at], at) + states_ref[0, at].astype(F32))
    leaving = [far_ref[:, piece:, :].reshape(wide, NSTATE).astype(F32)]
    for at in reversed(range(1, NEAR)):
        leaving.insert(0, faded(leaving[0], at) + states_ref[1, at].astype(F32))
    step_halves = halves(jnp.transpose(step))
    left_halves = halves(jnp.transpose(left))
    from_inflow = jnp.zeros((rows, tokens), F32)
    from_readout = jnp.zeros((rows, tokens), F32)
    meeting = jnp.zeros((rows, NSTATE), F32)
    for at in range(NEAR):
        segments = segment_matrix(rows, each, at)
        x, g, b, c = views(data_ref, at, wide)
        state = coming[at].astype(BF16)
        grad = leaving[at].astype(BF16)
        from_grad = dot(b, grad, 1, 1)
        from_state = dot(c, state, 1, 1)
        result_ref[at, :, :wide] = (
            spread(step_halves, segments)
            * (inner_ref[at].astype(F32) + spread(left_halves, segments) * from_grad)
        ).astype(BF16)
        result_ref[at, :, wide : wide + NSTATE] = (
            pair_ref[0, at].astype(F32) + dot(scaled_ref[0, at], grad, 1, 0)
        ).astype(BF16)
        result_ref[at, :, wide + NSTATE :] = (
            pair_ref[1, at].astype(F32) + dot(scaled_ref[1, at], state, 1, 0)
        ).astype(BF16)
        from_inflow = from_inflow + gathered(x.astype(F32) * from_grad, segments)
        from_readout = from_readout + gathered(g.astype(F32) * from_state, segments)
        high, low = halves(coming[at] * leaving[at])
        meeting = meeting + dot(segments, high, 1, 0) + dot(segments, low, 1, 0)
    inflow_part = left * from_inflow
    direct = sums_ref[1] + inflow_part
    of_total = jnp.sum(step * inflow_part, axis=1, keepdims=True) + shrink * jnp.sum(
        meeting, axis=1, keepdims=True
    )
    of_cumulated = sums_ref[0] + jnp.exp(cumulated) * from_readout - step * direct
    onward = jnp.where(iota((tokens, tokens), 0) >= iota((tokens, tokens), 1), 1.0, 0.0)
    of_decay = dot(of_cumulated, onward, 1, 0, EXACT) + of_total
    grad_step = direct - rate * of_decay
    sigmoid = 1.0 / (1.0 + jnp.exp(-preact))
    grad_pre = grad_step * sigmoid
    parts = pre_ref.shape[0] // NEAR
    for at in range(NEAR):
        rounded = grad_pre[at * each : (at + 1) * each].astype(BF16)
        for part in range(parts):
            pre_ref[at * parts + part] = rounded
    for shift in range(NEAR):
        own_refs[shift][...] = result_ref[lax.rem(place + shift, NEAR)]


def part_kernel(pre_ref, whole_ref, part_ref):
    parts, _, width = whole_ref.shape
    tokens = pre_ref.shape[2]
    each = pre_ref.shape[1]
    heads = NEAR * each
    group_place = lax.axis_index("head")
    grad_pre = jnp.concatenate(
        [pre_ref[near * parts + group_place].astype(F32) for near in range(NEAR)], axis=0
    ).astype(BF16)
    per = part_ref.shape[1]
    shards = heads // per
    size = LANES // shards
    shape = (heads, heads)
    swapped = iota(shape, 1) == shards * lax.rem(iota(shape, 0), per) + iota(shape, 0) // per
    swapped = dot(jnp.where(swapped, 1.0, 0.0).astype(BF16), grad_pre, 1, 0).astype(BF16)
    group = 8 // per
    block = iota((8, LANES), 1) // size
    row = iota((8, LANES), 0) // per
    masks = [
        jnp.logical_and(block == index, row == index % group) for index in range(shards)
    ]
    for source in range(parts):
        term = dot(swapped, whole_ref[source, :tokens, :], 1, 0)
        for index in range(width // LANES):
            lanes = slice(index * LANES, (index + 1) * LANES)
            turned = []
            for first in range(0, heads, 8):
                piece = term[first : first + 8, lanes]
                turned.append(
                    [piece] + [pltpu.roll(piece, size * turn, 1) for turn in range(1, shards)]
                )
            for shard in range(shards):
                packed = jnp.zeros((8, LANES), F32)
                for index2 in range(shards):
                    chosen = turned[index2 // group][(index2 - shard) % shards]
                    packed = jnp.where(masks[index2], chosen, packed)
                total_rows = packed[:per]
                for other in range(1, group):
                    total_rows = total_rows + packed[other * per : (other + 1) * per]
                where = (source * (width // LANES) + index) * shards + shard
                part_ref[where] = total_rows.astype(part_ref.dtype)


def input_kernel(pre_ref, whole_ref, out_ref):
    parts, _, width = whole_ref.shape
    tokens = pre_ref.shape[2]
    weights = whole_ref[:, tokens:, :]
    heads = weights.shape[1]
    pre = jnp.concatenate(
        [
            pre_ref[near * parts + part].astype(F32)
            for part in range(parts)
            for near in range(NEAR)
        ],
        axis=0,
    ).astype(BF16)
    out_ref[...] = dot(pre, weights.reshape(parts * heads, width), 0, 0).astype(BF16)


def final_kernel(*refs):
    received = refs[:NEAR]
    gx_ref, gb_ref, gc_ref = refs[NEAR:]
    wide = gx_ref.shape[1] // NEAR

    def fill(ref, quarter):
        gx_ref[:, quarter * wide : (quarter + 1) * wide] = ref[:, :wide]

    for shift, ref in enumerate(received):
        source = lax.rem(lax.rem(lax.axis_index("seq"), NEAR) + NEAR - shift, NEAR)
        for quarter in range(NEAR):
            pl.when(source == quarter)(lambda r=ref, q=quarter: fill(r, q))
    for out_ref, first in ((gb_ref, wide), (gc_ref, wide + NSTATE)):
        total = received[0][:, first : first + NSTATE].astype(F32)
        for ref in received[1:]:
            total = total + ref[:, first : first + NSTATE].astype(F32)
        out_ref[...] = total.astype(BF16)


def sum_kernel(part_ref, out_ref):
    heads, size = out_ref.shape
    total = jnp.sum(part_ref[...].astype(F32), axis=0)
    per = total.shape[0]
    shards = heads // per
    for shard in range(shards):
        piece = total[:, shard * size : (shard + 1) * size]
        for row in range(per):
            head = row * shards + shard
            out_ref[head : head + 1, :] = piece[row : row + 1, :]


def inside(value):
    return pltpu.with_memory_space_constraint(value, pltpu.VMEM)


def call(kernel, out_shape, *args, scratch=()):
    cost = pl.CostEstimate(flops=0, transcendentals=0, bytes_accessed=4_000_000)
    specs = [pl.BlockSpec(memory_space=pltpu.VMEM)] * len(args)
    return pl.pallas_call(
        kernel, out_shape=out_shape, in_specs=specs, scratch_shapes=scratch,
        cost_estimate=cost,
        compiler_params=pltpu.CompilerParams(vmem_limit_bytes=32 * 2**20),
    )(*args)


def outside(value):
    return pltpu.with_memory_space_constraint(value, pltpu.HBM)


def exchange(value, axis, groups=None):
    return inside(lax.all_to_all(value, axis, 0, 0, tiled=True, axis_index_groups=groups))


def body(
    layer_input, head_input, in_matrix, out_matrix, grad_output, step_weight, step_bias, decay_log
):
    parts = lax.axis_size("head")
    places = lax.axis_size("seq")
    shards = lax.axis_size("dp")
    tokens, width = layer_input.shape[1:]
    heads = step_weight.shape[1]
    runs = places // NEAR
    each = heads // NEAR
    rows = NEAR * each
    wide = each * P_SIZE
    count = NEAR * parts
    near = [[run * NEAR + at for at in range(NEAR)] for run in range(runs)]
    far = [[run * NEAR + at for run in range(runs)] for at in range(NEAR)]
    block = [[run * count + index for index in range(count)] for run in range(runs)]
    shape = pltpu.HBM
    local = pltpu.VMEM

    def turn(value, shift):
        pairs = [
            (run * NEAR + at, run * NEAR + (at + shift) % NEAR)
            for run in range(runs)
            for at in range(NEAR)
        ]
        return outside(lax.ppermute(value, "seq", pairs))

    x, b, c, g = head_input[0], in_matrix[0], out_matrix[0], grad_output[0]
    bias = step_bias.reshape(1, heads)
    logs = decay_log.reshape(1, heads)
    weight = step_weight.T
    packed = call(
        pack_kernel, shape((parts, tokens + heads, width), BF16), layer_input[0], weight
    )
    whole = lax.all_to_all(packed, "head", 0, 0, tiled=True)
    kept = outside(whole)
    data = call(
        data_kernel,
        (shape((tokens, 2 * wide + 2 * NSTATE), BF16),) * NEAR,
        x, g, b, c,
    )
    received = [data[0]] + [turn(data[shift], shift) for shift in range(1, NEAR)]
    terms = call(preact_kernel, local((NEAR, each, tokens), F32), whole, weight, bias)
    terms = exchange(terms, "seq", near)
    sent, data, small, states, scaled = call(
        state_kernel,
        (
            local((runs, 2 * wide // runs + EXTRA, NSTATE), BF16),
            local((NEAR, tokens, 2 * wide + 2 * NSTATE), BF16),
            local((4, rows, tokens), F32),
            local((2, NEAR, wide, NSTATE), BF16),
            local((2, NEAR, tokens, wide), BF16),
        ),
        terms, logs, *received,
    )
    sent = exchange(sent, "seq", far)
    inner, pair, sums = call(
        inner_kernel,
        (
            local((NEAR, tokens, wide), BF16),
            local((2, NEAR, tokens, NSTATE), BF16),
            local((2, rows, tokens), F32),
        ),
        data, small,
    )
    back = call(far_kernel, local((runs, 2 * wide // runs, NSTATE), BF16), sent)
    back = exchange(back, "seq", far)
    *owned, pre = call(
        last_kernel,
        (shape((tokens, wide + 2 * NSTATE), BF16),) * NEAR + (local((count, each, tokens), BF16),),
        back, data, small, states, scaled, inner, pair, sums,
        scratch=(pltpu.VMEM((NEAR, tokens, wide + 2 * NSTATE), BF16),),
    )
    pre = exchange(pre, ("seq", "head"), block)
    part = call(
        part_kernel,
        local((places * shards, heads // shards, LANES), BF16),
        pre, kept,
    )
    part = exchange(part, ("seq", "dp"))
    returned = [owned[0]]
    for shift in range(1, NEAR):
        returned.append(turn(owned[shift], shift))
    grad_input = call(input_kernel, shape((tokens, width), BF16), pre, kept)
    grad_x, grad_b, grad_c = call(
        final_kernel,
        (shape(x.shape, BF16), shape(b.shape, BF16), shape(c.shape, BF16)),
        *returned,
    )
    term = call(sum_kernel, shape((heads, LANES // shards), F32), part)
    return (grad_x[None], grad_b[None], grad_c[None], grad_input[None], term.T)


def solution(mesh):
    in_specs = (P("dp", "seq", "head"),) * 5 + (P(None, "head"), P("head"), P("head"))
    out_specs = (P("dp", "seq", "head"),) * 4 + (P(("seq", "dp"), "head"),)
    return jax.shard_map(body, mesh=mesh, in_specs=in_specs, out_specs=out_specs, check_vma=False)
```

```python
import jax
import jax.numpy as jnp
from jax import lax
from jax.experimental import pallas as pl
from jax.experimental.pallas import tpu as pltpu
from jax.sharding import PartitionSpec as P


P_SIZE = 64
NSTATE = 128
LANES = 128
NEAR = 4
EXTRA = 16
F32 = jnp.float32
BF16 = jnp.bfloat16
EXACT = lax.Precision.HIGHEST


def dot(a, b, ca, cb, precision=None):
    return lax.dot_general(
        a, b, (((ca,), (cb,)), ((), ())), preferred_element_type=F32, precision=precision
    )


def iota(shape, axis):
    return lax.broadcasted_iota(jnp.int32, shape, axis)


def halves(value):
    high = value.astype(BF16)
    return high, (value - high.astype(F32)).astype(BF16)


def thirds(value):
    first = value.astype(BF16).astype(F32)
    second = (value - first).astype(BF16).astype(F32)
    return first, second, value - first - second


def segment_matrix(rows, each, at):
    shape = (rows, each * P_SIZE)
    head = iota(shape, 0) - at * each
    lane = iota(shape, 1)
    inside = jnp.logical_and(lane >= head * P_SIZE, lane < head * P_SIZE + P_SIZE)
    return jnp.where(inside, 1.0, 0.0).astype(BF16)


def column(row, place, rows, each):
    size = row.shape[1]
    shape = (rows, size)
    mine = iota(shape, 1) == place * each + lax.rem(iota(shape, 0), each)
    return jnp.sum(jnp.where(mine, row, 0.0), axis=1, keepdims=True)


def spread(parts, segments):
    return dot(parts[0], segments, 1, 0) + dot(parts[1], segments, 1, 0)


def gathered(value, segments):
    high, low = halves(value)
    return dot(segments, high, 1, 1) + dot(segments, low, 1, 1)


def views(data_ref, at, wide):
    return (
        data_ref[at, :, :wide],
        data_ref[at, :, wide : 2 * wide],
        data_ref[at, :, 2 * wide : 2 * wide + NSTATE],
        data_ref[at, :, 2 * wide + NSTATE :],
    )


def pack_kernel(input_ref, weight_ref, out_ref):
    parts, _, width = out_ref.shape
    tokens = input_ref.shape[0]
    for part in range(parts):
        out_ref[part, :tokens, :] = input_ref[...]
        out_ref[part, tokens:, :] = weight_ref[:, part * width : (part + 1) * width]


def data_kernel(x_ref, g_ref, b_ref, c_ref, *out_refs):
    wide = x_ref.shape[1] // NEAR

    def fill(out_ref, quarter):
        lanes = slice(quarter * wide, (quarter + 1) * wide)
        out_ref[:, :wide] = x_ref[:, lanes]
        out_ref[:, wide : 2 * wide] = g_ref[:, lanes]

    for shift, out_ref in enumerate(out_refs):
        target = lax.rem(lax.rem(lax.axis_index("seq"), NEAR) + shift, NEAR)
        for quarter in range(NEAR):
            pl.when(target == quarter)(lambda o=out_ref, q=quarter: fill(o, q))
        out_ref[:, 2 * wide : 2 * wide + NSTATE] = b_ref[...]
        out_ref[:, 2 * wide + NSTATE :] = c_ref[...]


def preact_kernel(whole_ref, weight_ref, bias_ref, out_ref):
    parts, _, width = whole_ref.shape
    near, each, tokens = out_ref.shape
    term = column(bias_ref[...], 0, near * each, near * each)
    for part in range(parts):
        term = term + dot(
            weight_ref[:, part * width : (part + 1) * width], whole_ref[part, :tokens, :], 1, 1
        )
    out_ref[...] = term.reshape(near, each, tokens)


def state_kernel(terms_ref, log_ref, *refs):
    received = refs[:NEAR]
    sent_ref, data_ref, small_ref, states_ref, scaled_ref, arrived = refs[NEAR:]
    each, tokens = terms_ref.shape[1:]
    rows = NEAR * each
    wide = each * P_SIZE
    place = lax.rem(lax.axis_index("seq"), NEAR)
    copies = []
    for shift in range(NEAR):
        to = data_ref.at[lax.rem(place + NEAR - shift, NEAR)]
        copies.append(pltpu.make_async_copy(received[shift], to, arrived.at[shift]))
        copies[-1].start()
    preact = jnp.concatenate([terms_ref[at] for at in range(NEAR)], axis=0)
    tail = jnp.exp(-jnp.abs(preact))
    step = jnp.maximum(preact, 0.0) + jnp.log1p(tail)
    rate = jnp.exp(column(log_ref[...], place, rows, each))
    upto = jnp.where(iota((tokens, tokens), 0) <= iota((tokens, tokens), 1), 1.0, 0.0)
    cumulated = dot(-rate * step, upto, 1, 0, EXACT)
    total = cumulated[:, tokens - 1 :]
    small_ref[0] = preact
    small_ref[1] = step
    small_ref[2] = cumulated
    small_ref[3] = jnp.broadcast_to(rate, cumulated.shape)
    inflow = halves(jnp.transpose(jnp.exp(total - cumulated) * step))
    since = halves(jnp.transpose(jnp.exp(cumulated)))
    for copy in copies:
        copy.wait()
    for at in range(NEAR):
        segments = segment_matrix(rows, each, at)
        x, g, b, c = views(data_ref, at, wide)
        scaled = (x.astype(F32) * spread(inflow, segments)).astype(BF16)
        scaled_ref[0, at] = scaled
        states_ref[0, at] = dot(scaled, b, 0, 0).astype(BF16)
        scaled = (g.astype(F32) * spread(since, segments)).astype(BF16)
        scaled_ref[1, at] = scaled
        states_ref[1, at] = dot(scaled, c, 0, 0).astype(BF16)
    shrink = jnp.exp(total)
    slices = sent_ref.shape[0]
    piece = wide // slices
    line = iota((EXTRA, NSTATE), 0)
    for head in range(each):
        lines = slice(head * P_SIZE, (head + 1) * P_SIZE)
        factor = [shrink[at * each + head : at * each + head + 1] for at in range(NEAR)]
        both = []
        for which, order in ((0, range(NEAR)), (1, reversed(range(NEAR)))):
            state = None
            for at in order:
                here = states_ref[which, at, lines, :].astype(F32)
                state = here if state is None else factor[at] * state + here
            both.append(state)
        whole = factor[0]
        for at in range(1, NEAR):
            whole = whole * factor[at]
        first, second, third = thirds(whole)
        tile = jnp.where(line == 0, first, jnp.where(line == 1, second, third))
        tile = jnp.where(line < 3, tile, 0.0).astype(BF16)
        for part in range(P_SIZE // piece):
            index = head * (P_SIZE // piece) + part
            for which in range(2):
                sent_ref[index, which * piece : (which + 1) * piece, :] = both[which][
                    part * piece : (part + 1) * piece
                ].astype(BF16)
            sent_ref[index, 2 * piece :, :] = tile


def far_kernel(states_ref, out_ref):
    count, rows2, _ = out_ref.shape
    rows = rows2 // 2
    shrink = [
        jnp.sum(states_ref[at, rows2 : rows2 + 3, :].astype(F32), axis=0, keepdims=True)
        for at in range(count)
    ]
    for start, order in ((0, range(count)), (rows, reversed(range(count)))):
        state = jnp.zeros((rows, NSTATE), F32)
        for at in order:
            out_ref[at, start : start + rows, :] = state.astype(BF16)
            state = shrink[at] * state + states_ref[at, start : start + rows, :].astype(F32)


def inner_kernel(data_ref, small_ref, inner_ref, pair_ref, sums_ref):
    _, rows, tokens = small_ref.shape
    each = rows // NEAR
    wide = each * P_SIZE
    cumulated = small_ref[2]
    step_column = jnp.transpose(small_ref[1])
    cumulated_column = jnp.transpose(cumulated)
    allowed = iota((tokens, tokens), 0) <= iota((tokens, tokens), 1)
    lower = iota((tokens, LANES), 1) < P_SIZE
    zero = jnp.zeros((tokens, LANES), BF16)
    row_sums = []
    direct = jnp.zeros((rows, tokens), F32)
    for at in range(NEAR):
        x_all, g_all, b, c = views(data_ref, at, wide)
        kernel = dot(b, c, 1, 1)
        d_kernel = jnp.zeros((tokens, tokens), F32)
        products = []
        for pair in range(each // 2):
            lanes = slice(pair * LANES, (pair + 1) * LANES)
            x = x_all[:, lanes]
            g = g_all[:, lanes]
            both = []
            for half in range(2):
                row = at * each + 2 * pair + half
                span = cumulated[row : row + 1, :] - cumulated_column[:, row : row + 1]
                span = jnp.exp(jnp.where(allowed, span, -1e30))
                mine = jnp.where(lower, x, zero) if half == 0 else jnp.where(lower, zero, x)
                product = dot(mine, g, 1, 1) * span * step_column[:, row : row + 1]
                d_kernel = d_kernel + product
                row_sums.append(jnp.sum(product * kernel, axis=0, keepdims=True))
                both.append(dot((span * kernel).astype(BF16), g, 1, 0))
            inner = jnp.where(lower, both[0], both[1])
            inner_ref[at, :, lanes] = inner.astype(BF16)
            products.append(x.astype(F32) * inner)
        d_kernel = d_kernel.astype(BF16)
        pair_ref[0, at] = dot(d_kernel, c, 1, 0).astype(BF16)
        pair_ref[1, at] = dot(d_kernel, b, 0, 0).astype(BF16)
        direct = direct + gathered(
            jnp.concatenate(products, axis=1), segment_matrix(rows, each, at)
        )
    sums_ref[0] = jnp.concatenate(row_sums, axis=0)
    sums_ref[1] = direct


def last_kernel(
    far_ref, data_ref, small_ref, states_ref, scaled_ref, inner_ref, pairs_ref,
    sums_ref, kept_ref, *refs
):
    own_refs = refs[:NEAR]
    pre_ref, whole_ref, result_ref, pair_ref, arrived = refs[NEAR:]
    pairs = pltpu.make_async_copy(pairs_ref, pair_ref, arrived.at[0])
    pairs.start()
    fetch = pltpu.make_async_copy(kept_ref, whole_ref, arrived.at[1])
    fetch.start()
    _, rows, tokens = small_ref.shape
    each = rows // NEAR
    wide = each * P_SIZE
    place = lax.rem(lax.axis_index("seq"), NEAR)
    preact = small_ref[0]
    step = small_ref[1]
    cumulated = small_ref[2]
    total = cumulated[:, tokens - 1 :]
    shrink = jnp.exp(total)
    rate = small_ref[3]
    left = jnp.exp(total - cumulated)
    piece = far_ref.shape[1] // 2

    def faded(state, at):
        return jnp.concatenate(
            [
                shrink[at * each + head : at * each + head + 1]
                * state[head * P_SIZE : (head + 1) * P_SIZE]
                for head in range(each)
            ],
            axis=0,
        )

    coming = [far_ref[:, :piece, :].reshape(wide, NSTATE).astype(F32)]
    for at in range(NEAR - 1):
        coming.append(faded(coming[at], at) + states_ref[0, at].astype(F32))
    leaving = [far_ref[:, piece:, :].reshape(wide, NSTATE).astype(F32)]
    for at in reversed(range(1, NEAR)):
        leaving.insert(0, faded(leaving[0], at) + states_ref[1, at].astype(F32))
    step_halves = halves(jnp.transpose(step))
    left_halves = halves(jnp.transpose(left))
    from_inflow = jnp.zeros((rows, tokens), F32)
    from_readout = jnp.zeros((rows, tokens), F32)
    meeting = jnp.zeros((rows, NSTATE), F32)
    for at in range(NEAR):
        segments = segment_matrix(rows, each, at)
        x, g, b, c = views(data_ref, at, wide)
        state = coming[at].astype(BF16)
        grad = leaving[at].astype(BF16)
        from_grad = dot(b, grad, 1, 1)
        from_state = dot(c, state, 1, 1)
        result_ref[at, :, :wide] = (
            spread(step_halves, segments)
            * (inner_ref[at].astype(F32) + spread(left_halves, segments) * from_grad)
        ).astype(BF16)
        from_inflow = from_inflow + gathered(x.astype(F32) * from_grad, segments)
        from_readout = from_readout + gathered(g.astype(F32) * from_state, segments)
        high, low = halves(coming[at] * leaving[at])
        meeting = meeting + dot(segments, high, 1, 0) + dot(segments, low, 1, 0)
    inflow_part = left * from_inflow
    direct = sums_ref[1] + inflow_part
    of_total = jnp.sum(step * inflow_part, axis=1, keepdims=True) + shrink * jnp.sum(
        meeting, axis=1, keepdims=True
    )
    of_cumulated = sums_ref[0] + jnp.exp(cumulated) * from_readout - step * direct
    onward = jnp.where(iota((tokens, tokens), 0) >= iota((tokens, tokens), 1), 1.0, 0.0)
    of_decay = dot(of_cumulated, onward, 1, 0, EXACT) + of_total
    grad_step = direct - rate * of_decay
    sigmoid = 1.0 / (1.0 + jnp.exp(-preact))
    grad_pre = grad_step * sigmoid
    parts = pre_ref.shape[0] // NEAR
    for at in range(NEAR):
        rounded = grad_pre[at * each : (at + 1) * each].astype(BF16)
        for part in range(parts):
            pre_ref[at * parts + part] = rounded
    pairs.wait()
    for at in range(NEAR):
        for which, of_state in ((0, leaving[at]), (1, coming[at])):
            first = wide + which * NSTATE
            result_ref[at, :, first : first + NSTATE] = (
                pair_ref[which, at].astype(F32)
                + dot(scaled_ref[which, at], of_state.astype(BF16), 1, 0)
            ).astype(BF16)
    for shift in range(NEAR):
        own_refs[shift][...] = result_ref[lax.rem(place + shift, NEAR)]
    fetch.wait()


def part_kernel(pre_ref, whole_ref, part_ref):
    parts, _, width = whole_ref.shape
    tokens = pre_ref.shape[2]
    each = pre_ref.shape[1]
    heads = NEAR * each
    group_place = lax.axis_index("head")
    grad_pre = jnp.concatenate(
        [pre_ref[near * parts + group_place].astype(F32) for near in range(NEAR)], axis=0
    ).astype(BF16)
    per = part_ref.shape[1]
    shards = heads // per
    size = LANES // shards
    shape = (heads, heads)
    swapped = iota(shape, 1) == shards * lax.rem(iota(shape, 0), per) + iota(shape, 0) // per
    swapped = dot(jnp.where(swapped, 1.0, 0.0).astype(BF16), grad_pre, 1, 0).astype(BF16)
    group = 8 // per
    block = iota((8, LANES), 1) // size
    row = iota((8, LANES), 0) // per
    masks = [
        jnp.logical_and(block == index, row == index % group) for index in range(shards)
    ]
    for source in range(parts):
        term = dot(swapped, whole_ref[source, :tokens, :], 1, 0)
        for index in range(width // LANES):
            lanes = slice(index * LANES, (index + 1) * LANES)
            turned = []
            for first in range(0, heads, 8):
                piece = term[first : first + 8, lanes]
                turned.append(
                    [piece] + [pltpu.roll(piece, size * turn, 1) for turn in range(1, shards)]
                )
            for shard in range(shards):
                packed = jnp.zeros((8, LANES), F32)
                for index2 in range(shards):
                    chosen = turned[index2 // group][(index2 - shard) % shards]
                    packed = jnp.where(masks[index2], chosen, packed)
                total_rows = packed[:per]
                for other in range(1, group):
                    total_rows = total_rows + packed[other * per : (other + 1) * per]
                where = (source * (width // LANES) + index) * shards + shard
                part_ref[where] = total_rows.astype(part_ref.dtype)


def input_kernel(pre_ref, whole_ref, out_ref):
    parts, _, width = whole_ref.shape
    tokens = pre_ref.shape[2]
    weights = whole_ref[:, tokens:, :]
    heads = weights.shape[1]
    pre = jnp.concatenate(
        [
            pre_ref[near * parts + part].astype(F32)
            for part in range(parts)
            for near in range(NEAR)
        ],
        axis=0,
    ).astype(BF16)
    out_ref[...] = dot(pre, weights.reshape(parts * heads, width), 0, 0).astype(BF16)


def final_kernel(*refs):
    received = refs[:NEAR]
    gx_ref, gb_ref, gc_ref = refs[NEAR:]
    wide = gx_ref.shape[1] // NEAR

    def fill(ref, quarter):
        gx_ref[:, quarter * wide : (quarter + 1) * wide] = ref[:, :wide]

    for shift, ref in enumerate(received):
        source = lax.rem(lax.rem(lax.axis_index("seq"), NEAR) + NEAR - shift, NEAR)
        for quarter in range(NEAR):
            pl.when(source == quarter)(lambda r=ref, q=quarter: fill(r, q))
    for out_ref, first in ((gb_ref, wide), (gc_ref, wide + NSTATE)):
        total = received[0][:, first : first + NSTATE].astype(F32)
        for ref in received[1:]:
            total = total + ref[:, first : first + NSTATE].astype(F32)
        out_ref[...] = total.astype(BF16)


def sum_kernel(part_ref, out_ref):
    heads, size = out_ref.shape
    total = jnp.sum(part_ref[...].astype(F32), axis=0)
    per = total.shape[0]
    shards = heads // per
    for shard in range(shards):
        piece = total[:, shard * size : (shard + 1) * size]
        for row in range(per):
            head = row * shards + shard
            out_ref[head : head + 1, :] = piece[row : row + 1, :]


def inside(value):
    return pltpu.with_memory_space_constraint(value, pltpu.VMEM)


def call(kernel, out_shape, *args, scratch=(), far={}):
    cost = pl.CostEstimate(flops=0, transcendentals=0, bytes_accessed=4_000_000)
    specs = [
        pl.BlockSpec(memory_space=far.get(index, pltpu.VMEM))
        for index in range(len(args))
    ]
    return pl.pallas_call(
        kernel, out_shape=out_shape, in_specs=specs, scratch_shapes=scratch,
        cost_estimate=cost,
        compiler_params=pltpu.CompilerParams(vmem_limit_bytes=32 * 2**20),
    )(*args)


def outside(value):
    return pltpu.with_memory_space_constraint(value, pltpu.HBM)


def exchange(value, axis, groups=None):
    return inside(lax.all_to_all(value, axis, 0, 0, tiled=True, axis_index_groups=groups))


def body(
    layer_input, head_input, in_matrix, out_matrix, grad_output, step_weight, step_bias, decay_log
):
    parts = lax.axis_size("head")
    places = lax.axis_size("seq")
    shards = lax.axis_size("dp")
    tokens, width = layer_input.shape[1:]
    heads = step_weight.shape[1]
    runs = places // NEAR
    each = heads // NEAR
    rows = NEAR * each
    wide = each * P_SIZE
    count = NEAR * parts
    near = [[run * NEAR + at for at in range(NEAR)] for run in range(runs)]
    far = [[run * NEAR + at for run in range(runs)] for at in range(NEAR)]
    block = [[run * count + index for index in range(count)] for run in range(runs)]
    shape = pltpu.HBM
    local = pltpu.VMEM

    def turn(value, shift):
        pairs = [
            (run * NEAR + at, run * NEAR + (at + shift) % NEAR)
            for run in range(runs)
            for at in range(NEAR)
        ]
        return lax.ppermute(value, "seq", pairs)

    x, b, c, g = head_input[0], in_matrix[0], out_matrix[0], grad_output[0]
    bias = step_bias.reshape(1, heads)
    logs = decay_log.reshape(1, heads)
    weight = step_weight.T
    packed = call(
        pack_kernel, shape((parts, tokens + heads, width), BF16),
        outside(layer_input[0]), outside(weight),
    )
    whole = lax.all_to_all(packed, "head", 0, 0, tiled=True)
    kept = outside(whole)
    data = call(
        data_kernel,
        (shape((tokens, 2 * wide + 2 * NSTATE), BF16),) * NEAR,
        x, g, b, c,
    )
    received = [outside(data[0])]
    received += [outside(turn(data[shift], shift)) for shift in range(1, NEAR)]
    terms = call(preact_kernel, local((NEAR, each, tokens), F32), whole, weight, bias)
    terms = exchange(terms, "seq", near)
    sent, data, small, states, scaled = call(
        state_kernel,
        (
            local((runs, 2 * wide // runs + EXTRA, NSTATE), BF16),
            local((NEAR, tokens, 2 * wide + 2 * NSTATE), BF16),
            local((4, rows, tokens), F32),
            local((2, NEAR, wide, NSTATE), BF16),
            local((2, NEAR, tokens, wide), BF16),
        ),
        terms, logs, *received, far={index: pltpu.HBM for index in range(2, 2 + NEAR)},
        scratch=(pltpu.SemaphoreType.DMA((NEAR,)),),
    )
    sent = exchange(sent, "seq", far)
    inner, pair, sums = call(
        inner_kernel,
        (
            local((NEAR, tokens, wide), BF16),
            shape((2, NEAR, tokens, NSTATE), BF16),
            local((2, rows, tokens), F32),
        ),
        data, small,
    )
    back = call(far_kernel, local((runs, 2 * wide // runs, NSTATE), BF16), sent)
    back = exchange(back, "seq", far)
    *owned, pre, whole = call(
        last_kernel,
        (shape((tokens, wide + 2 * NSTATE), BF16),) * NEAR + (
            local((count, each, tokens), BF16), local(whole.shape, BF16),
        ),
        back, data, small, states, scaled, inner, outside(pair), sums, kept, far={6: pltpu.HBM, 8: pltpu.HBM},
        scratch=(
            pltpu.VMEM((NEAR, tokens, wide + 2 * NSTATE), BF16),
            pltpu.VMEM(pair.shape, BF16),
            pltpu.SemaphoreType.DMA((2,)),
        ),
    )
    pre = exchange(pre, ("seq", "head"), block)
    part = call(
        part_kernel,
        local((places * shards, heads // shards, LANES), BF16),
        pre, whole,
    )
    part = exchange(part, ("seq", "dp"))
    returned = [owned[0]]
    for shift in range(1, NEAR):
        returned.append(turn(owned[shift], shift))
    grad_input = call(input_kernel, shape((tokens, width), BF16), pre, whole)
    grad_x, grad_b, grad_c = call(
        final_kernel,
        (shape(x.shape, BF16), shape(b.shape, BF16), shape(c.shape, BF16)),
        *returned,
    )
    term = call(sum_kernel, shape((heads, LANES // shards), F32), part)
    return (grad_x[None], grad_b[None], grad_c[None], grad_input[None], term.T)


def solution(mesh):
    in_specs = (P("dp", "seq", "head"),) * 5 + (P(None, "head"), P("head"), P("head"))
    out_specs = (P("dp", "seq", "head"),) * 4 + (P(("seq", "dp"), "head"),)
    return jax.shard_map(body, mesh=mesh, in_specs=in_specs, out_specs=out_specs, check_vma=False)
```

```python
import jax
import jax.numpy as jnp
from jax import lax
from jax.experimental import pallas as pl
from jax.experimental.pallas import tpu as pltpu
from jax.sharding import PartitionSpec as P


P_SIZE = 64
NSTATE = 128
LANES = 128
NEAR = 4
EXTRA = 8
F32 = jnp.float32
BF16 = jnp.bfloat16
EXACT = lax.Precision.HIGHEST


def dot(a, b, ca, cb, precision=None):
    return lax.dot_general(
        a, b, (((ca,), (cb,)), ((), ())), preferred_element_type=F32, precision=precision
    )


def iota(shape, axis):
    return lax.broadcasted_iota(jnp.int32, shape, axis)


def halves(value):
    high = value.astype(BF16)
    return high, (value - high.astype(F32)).astype(BF16)


def thirds(value):
    first = value.astype(BF16).astype(F32)
    second = (value - first).astype(BF16).astype(F32)
    return first, second, value - first - second


def segment_matrix(rows, each, at):
    shape = (rows, each * P_SIZE)
    head = iota(shape, 0) - at * each
    lane = iota(shape, 1)
    inside = jnp.logical_and(lane >= head * P_SIZE, lane < head * P_SIZE + P_SIZE)
    return jnp.where(inside, 1.0, 0.0).astype(BF16)


def column(row, place, rows, each):
    size = row.shape[1]
    shape = (rows, size)
    mine = iota(shape, 1) == place * each + lax.rem(iota(shape, 0), each)
    return jnp.sum(jnp.where(mine, row, 0.0), axis=1, keepdims=True)


def spread(parts, segments):
    return dot(parts[0], segments, 1, 0) + dot(parts[1], segments, 1, 0)


def gathered(value, segments):
    high, low = halves(value)
    return dot(segments, high, 1, 1) + dot(segments, low, 1, 1)


def views(data_ref, at, wide):
    return (
        data_ref[at, :, :wide],
        data_ref[at, :, wide : 2 * wide],
        data_ref[at, :, 2 * wide : 2 * wide + NSTATE],
        data_ref[at, :, 2 * wide + NSTATE :],
    )


def pack_kernel(input_ref, weight_ref, out_ref):
    parts, _, width = out_ref.shape
    tokens = input_ref.shape[0]
    for part in range(parts):
        out_ref[part, :tokens, :] = input_ref[...]
        out_ref[part, tokens:, :] = weight_ref[:, part * width : (part + 1) * width]


def data_kernel(x_ref, g_ref, b_ref, c_ref, *out_refs):
    wide = x_ref.shape[1] // NEAR

    def fill(out_ref, quarter):
        lanes = slice(quarter * wide, (quarter + 1) * wide)
        out_ref[:, :wide] = x_ref[:, lanes]
        out_ref[:, wide : 2 * wide] = g_ref[:, lanes]

    for shift, out_ref in enumerate(out_refs):
        target = lax.rem(lax.rem(lax.axis_index("seq"), NEAR) + shift, NEAR)
        for quarter in range(NEAR):
            pl.when(target == quarter)(lambda o=out_ref, q=quarter: fill(o, q))
        out_ref[:, 2 * wide : 2 * wide + NSTATE] = b_ref[...]
        out_ref[:, 2 * wide + NSTATE :] = c_ref[...]


def preact_kernel(whole_ref, weight_ref, bias_ref, out_ref):
    parts, _, width = whole_ref.shape
    near, each, tokens = out_ref.shape
    term = column(bias_ref[...], 0, near * each, near * each)
    for part in range(parts):
        term = term + dot(
            weight_ref[:, part * width : (part + 1) * width], whole_ref[part, :tokens, :], 1, 1
        )
    out_ref[...] = term.reshape(near, each, tokens)


def state_kernel(terms_ref, log_ref, *refs):
    received = refs[:NEAR]
    sent_ref, data_ref, small_ref, states_ref, scaled_ref, arrived = refs[NEAR:]
    each, tokens = terms_ref.shape[1:]
    rows = NEAR * each
    wide = each * P_SIZE
    place = lax.rem(lax.axis_index("seq"), NEAR)
    copies = []
    for shift in range(NEAR):
        to = data_ref.at[lax.rem(place + NEAR - shift, NEAR)]
        copies.append(pltpu.make_async_copy(received[shift], to, arrived.at[shift]))
        copies[-1].start()
    preact = jnp.concatenate([terms_ref[at] for at in range(NEAR)], axis=0)
    tail = jnp.exp(-jnp.abs(preact))
    step = jnp.maximum(preact, 0.0) + jnp.log1p(tail)
    rate = jnp.exp(column(log_ref[...], place, rows, each))
    upto = jnp.where(iota((tokens, tokens), 0) <= iota((tokens, tokens), 1), 1.0, 0.0)
    cumulated = dot(-rate * step, upto, 1, 0, EXACT)
    total = cumulated[:, tokens - 1 :]
    small_ref[0] = preact
    small_ref[1] = step
    small_ref[2] = cumulated
    small_ref[3] = jnp.broadcast_to(rate, cumulated.shape)
    inflow = halves(jnp.transpose(jnp.exp(total - cumulated) * step))
    since = halves(jnp.transpose(jnp.exp(cumulated)))
    for copy in copies:
        copy.wait()
    for at in range(NEAR):
        segments = segment_matrix(rows, each, at)
        x, g, b, c = views(data_ref, at, wide)
        scaled = (x.astype(F32) * spread(inflow, segments)).astype(BF16)
        scaled_ref[0, at] = scaled
        states_ref[0, at] = dot(scaled, b, 0, 0).astype(BF16)
        scaled = (g.astype(F32) * spread(since, segments)).astype(BF16)
        scaled_ref[1, at] = scaled
        states_ref[1, at] = dot(scaled, c, 0, 0).astype(BF16)
    shrink = jnp.exp(total)
    slices = sent_ref.shape[0]
    piece = wide // slices
    line = iota((EXTRA, NSTATE), 0)
    for head in range(each):
        lines = slice(head * P_SIZE, (head + 1) * P_SIZE)
        factor = [shrink[at * each + head : at * each + head + 1] for at in range(NEAR)]
        both = []
        for which, order in ((0, range(NEAR)), (1, reversed(range(NEAR)))):
            state = None
            for at in order:
                here = states_ref[which, at, lines, :].astype(F32)
                state = here if state is None else factor[at] * state + here
            both.append(state)
        whole = factor[0]
        for at in range(1, NEAR):
            whole = whole * factor[at]
        first, second, third = thirds(whole)
        tile = jnp.where(line == 0, first, jnp.where(line == 1, second, third))
        tile = jnp.where(line < 3, tile, 0.0).astype(BF16)
        for part in range(P_SIZE // piece):
            index = head * (P_SIZE // piece) + part
            for which in range(2):
                sent_ref[index, which * piece : (which + 1) * piece, :] = both[which][
                    part * piece : (part + 1) * piece
                ].astype(BF16)
            sent_ref[index, 2 * piece :, :] = tile


def far_kernel(states_ref, out_ref):
    count, rows2, _ = out_ref.shape
    rows = rows2 // 2
    shrink = [
        jnp.sum(states_ref[at, rows2 : rows2 + 3, :].astype(F32), axis=0, keepdims=True)
        for at in range(count)
    ]
    for start, order in ((0, range(count)), (rows, reversed(range(count)))):
        state = jnp.zeros((rows, NSTATE), F32)
        for at in order:
            out_ref[at, start : start + rows, :] = state.astype(BF16)
            state = shrink[at] * state + states_ref[at, start : start + rows, :].astype(F32)


def inner_kernel(data_ref, small_ref, inner_ref, pair_ref, sums_ref):
    _, rows, tokens = small_ref.shape
    each = rows // NEAR
    wide = each * P_SIZE
    cumulated = small_ref[2]
    step_column = jnp.transpose(small_ref[1])
    cumulated_column = jnp.transpose(cumulated)
    allowed = iota((tokens, tokens), 0) <= iota((tokens, tokens), 1)
    lower = iota((tokens, LANES), 1) < P_SIZE
    zero = jnp.zeros((tokens, LANES), BF16)
    row_sums = []
    direct = jnp.zeros((rows, tokens), F32)
    for at in range(NEAR):
        x_all, g_all, b, c = views(data_ref, at, wide)
        kernel = dot(b, c, 1, 1)
        d_kernel = jnp.zeros((tokens, tokens), F32)
        products = []
        for pair in range(each // 2):
            lanes = slice(pair * LANES, (pair + 1) * LANES)
            x = x_all[:, lanes]
            g = g_all[:, lanes]
            both = []
            for half in range(2):
                row = at * each + 2 * pair + half
                span = cumulated[row : row + 1, :] - cumulated_column[:, row : row + 1]
                span = jnp.exp(jnp.where(allowed, span, -1e30))
                mine = jnp.where(lower, x, zero) if half == 0 else jnp.where(lower, zero, x)
                product = dot(mine, g, 1, 1) * span * step_column[:, row : row + 1]
                d_kernel = d_kernel + product
                row_sums.append(jnp.sum(product * kernel, axis=0, keepdims=True))
                both.append(dot((span * kernel).astype(BF16), g, 1, 0))
            inner = jnp.where(lower, both[0], both[1])
            inner_ref[at, :, lanes] = inner.astype(BF16)
            products.append(x.astype(F32) * inner)
        d_kernel = d_kernel.astype(BF16)
        pair_ref[0, at] = dot(d_kernel, c, 1, 0).astype(BF16)
        pair_ref[1, at] = dot(d_kernel, b, 0, 0).astype(BF16)
        direct = direct + gathered(
            jnp.concatenate(products, axis=1), segment_matrix(rows, each, at)
        )
    sums_ref[0] = jnp.concatenate(row_sums, axis=0)
    sums_ref[1] = direct


def last_kernel(
    far_ref, data_ref, small_ref, states_ref, scaled_ref, inner_ref, pairs_ref,
    sums_ref, kept_ref, *refs
):
    own_refs = refs[:NEAR]
    pre_ref, whole_ref, result_ref, pair_ref, arrived = refs[NEAR:]
    pairs = pltpu.make_async_copy(pairs_ref, pair_ref, arrived.at[0])
    pairs.start()
    fetch = pltpu.make_async_copy(kept_ref, whole_ref, arrived.at[1])
    fetch.start()
    _, rows, tokens = small_ref.shape
    each = rows // NEAR
    wide = each * P_SIZE
    place = lax.rem(lax.axis_index("seq"), NEAR)
    preact = small_ref[0]
    step = small_ref[1]
    cumulated = small_ref[2]
    total = cumulated[:, tokens - 1 :]
    shrink = jnp.exp(total)
    rate = small_ref[3]
    left = jnp.exp(total - cumulated)
    piece = far_ref.shape[1] // 2

    def faded(state, at):
        return jnp.concatenate(
            [
                shrink[at * each + head : at * each + head + 1]
                * state[head * P_SIZE : (head + 1) * P_SIZE]
                for head in range(each)
            ],
            axis=0,
        )

    coming = [far_ref[:, :piece, :].reshape(wide, NSTATE).astype(F32)]
    for at in range(NEAR - 1):
        coming.append(faded(coming[at], at) + states_ref[0, at].astype(F32))
    leaving = [far_ref[:, piece:, :].reshape(wide, NSTATE).astype(F32)]
    for at in reversed(range(1, NEAR)):
        leaving.insert(0, faded(leaving[0], at) + states_ref[1, at].astype(F32))
    step_halves = halves(jnp.transpose(step))
    left_halves = halves(jnp.transpose(left))
    from_inflow = jnp.zeros((rows, tokens), F32)
    from_readout = jnp.zeros((rows, tokens), F32)
    meeting = jnp.zeros((rows, NSTATE), F32)
    for at in range(NEAR):
        segments = segment_matrix(rows, each, at)
        x, g, b, c = views(data_ref, at, wide)
        state = coming[at].astype(BF16)
        grad = leaving[at].astype(BF16)
        from_grad = dot(b, grad, 1, 1)
        from_state = dot(c, state, 1, 1)
        result_ref[at, :, :wide] = (
            spread(step_halves, segments)
            * (inner_ref[at].astype(F32) + spread(left_halves, segments) * from_grad)
        ).astype(BF16)
        from_inflow = from_inflow + gathered(x.astype(F32) * from_grad, segments)
        from_readout = from_readout + gathered(g.astype(F32) * from_state, segments)
        high, low = halves(coming[at] * leaving[at])
        meeting = meeting + dot(segments, high, 1, 0) + dot(segments, low, 1, 0)
    inflow_part = left * from_inflow
    direct = sums_ref[1] + inflow_part
    of_total = jnp.sum(step * inflow_part, axis=1, keepdims=True) + shrink * jnp.sum(
        meeting, axis=1, keepdims=True
    )
    of_cumulated = sums_ref[0] + jnp.exp(cumulated) * from_readout - step * direct
    onward = jnp.where(iota((tokens, tokens), 0) >= iota((tokens, tokens), 1), 1.0, 0.0)
    of_decay = dot(of_cumulated, onward, 1, 0, EXACT) + of_total
    grad_step = direct - rate * of_decay
    sigmoid = 1.0 / (1.0 + jnp.exp(-preact))
    grad_pre = grad_step * sigmoid
    parts = pre_ref.shape[0] // NEAR
    for at in range(NEAR):
        rounded = grad_pre[at * each : (at + 1) * each].astype(BF16)
        for part in range(parts):
            pre_ref[at * parts + part] = rounded
    pairs.wait()
    for at in range(NEAR):
        for which, of_state in ((0, leaving[at]), (1, coming[at])):
            first = wide + which * NSTATE
            result_ref[at, :, first : first + NSTATE] = (
                pair_ref[which, at].astype(F32)
                + dot(scaled_ref[which, at], of_state.astype(BF16), 1, 0)
            ).astype(BF16)
    for shift in range(NEAR):
        own_refs[shift][...] = result_ref[lax.rem(place + shift, NEAR)]
    fetch.wait()


def part_kernel(pre_ref, whole_ref, part_ref):
    parts, _, width = whole_ref.shape
    tokens = pre_ref.shape[2]
    each = pre_ref.shape[1]
    heads = NEAR * each
    group_place = lax.axis_index("head")
    grad_pre = jnp.concatenate(
        [pre_ref[near * parts + group_place].astype(F32) for near in range(NEAR)], axis=0
    ).astype(BF16)
    per = part_ref.shape[1]
    shards = heads // per
    size = LANES // shards
    shape = (heads, heads)
    swapped = iota(shape, 1) == shards * lax.rem(iota(shape, 0), per) + iota(shape, 0) // per
    swapped = dot(jnp.where(swapped, 1.0, 0.0).astype(BF16), grad_pre, 1, 0).astype(BF16)
    group = 8 // per
    block = iota((8, LANES), 1) // size
    row = iota((8, LANES), 0) // per
    masks = [
        jnp.logical_and(block == index, row == index % group) for index in range(shards)
    ]
    for source in range(parts):
        term = dot(swapped, whole_ref[source, :tokens, :], 1, 0)
        for index in range(width // LANES):
            lanes = slice(index * LANES, (index + 1) * LANES)
            turned = []
            for first in range(0, heads, 8):
                piece = term[first : first + 8, lanes]
                turned.append(
                    [piece] + [pltpu.roll(piece, size * turn, 1) for turn in range(1, shards)]
                )
            for shard in range(shards):
                packed = jnp.zeros((8, LANES), F32)
                for index2 in range(shards):
                    chosen = turned[index2 // group][(index2 - shard) % shards]
                    packed = jnp.where(masks[index2], chosen, packed)
                total_rows = packed[:per]
                for other in range(1, group):
                    total_rows = total_rows + packed[other * per : (other + 1) * per]
                where = (source * (width // LANES) + index) * shards + shard
                part_ref[where] = total_rows.astype(part_ref.dtype)


def input_kernel(pre_ref, whole_ref, out_ref):
    parts, _, width = whole_ref.shape
    tokens = pre_ref.shape[2]
    weights = whole_ref[:, tokens:, :]
    heads = weights.shape[1]
    pre = jnp.concatenate(
        [
            pre_ref[near * parts + part].astype(F32)
            for part in range(parts)
            for near in range(NEAR)
        ],
        axis=0,
    ).astype(BF16)
    out_ref[...] = dot(pre, weights.reshape(parts * heads, width), 0, 0).astype(BF16)


def final_kernel(term_ref, *refs):
    del term_ref
    received = refs[:NEAR]
    gx_ref, gb_ref, gc_ref = refs[NEAR:]
    wide = gx_ref.shape[1] // NEAR

    def fill(ref, quarter):
        gx_ref[:, quarter * wide : (quarter + 1) * wide] = ref[:, :wide]

    for shift, ref in enumerate(received):
        source = lax.rem(lax.rem(lax.axis_index("seq"), NEAR) + NEAR - shift, NEAR)
        for quarter in range(NEAR):
            pl.when(source == quarter)(lambda r=ref, q=quarter: fill(r, q))
    for out_ref, first in ((gb_ref, wide), (gc_ref, wide + NSTATE)):
        total = received[0][:, first : first + NSTATE].astype(F32)
        for ref in received[1:]:
            total = total + ref[:, first : first + NSTATE].astype(F32)
        out_ref[...] = total.astype(BF16)


def sum_kernel(part_ref, out_ref):
    heads, size = out_ref.shape
    total = jnp.sum(part_ref[...].astype(F32), axis=0)
    per = total.shape[0]
    shards = heads // per
    for shard in range(shards):
        piece = total[:, shard * size : (shard + 1) * size]
        for row in range(per):
            head = row * shards + shard
            out_ref[head : head + 1, :] = piece[row : row + 1, :]


def inside(value):
    return pltpu.with_memory_space_constraint(value, pltpu.VMEM)


def call(kernel, out_shape, *args, scratch=(), far={}):
    cost = pl.CostEstimate(flops=0, transcendentals=0, bytes_accessed=4_000_000)
    specs = [
        pl.BlockSpec(memory_space=far.get(index, pltpu.VMEM))
        for index in range(len(args))
    ]
    return pl.pallas_call(
        kernel, out_shape=out_shape, in_specs=specs, scratch_shapes=scratch,
        cost_estimate=cost,
        compiler_params=pltpu.CompilerParams(vmem_limit_bytes=32 * 2**20),
    )(*args)


def outside(value):
    return pltpu.with_memory_space_constraint(value, pltpu.HBM)


def exchange(value, axis, groups=None):
    return inside(lax.all_to_all(value, axis, 0, 0, tiled=True, axis_index_groups=groups))


def body(
    layer_input, head_input, in_matrix, out_matrix, grad_output, step_weight, step_bias, decay_log
):
    parts = lax.axis_size("head")
    places = lax.axis_size("seq")
    shards = lax.axis_size("dp")
    tokens, width = layer_input.shape[1:]
    heads = step_weight.shape[1]
    runs = places // NEAR
    each = heads // NEAR
    rows = NEAR * each
    wide = each * P_SIZE
    count = NEAR * parts
    near = [[run * NEAR + at for at in range(NEAR)] for run in range(runs)]
    far = [[run * NEAR + at for run in range(runs)] for at in range(NEAR)]
    block = [[run * count + index for index in range(count)] for run in range(runs)]
    shape = pltpu.HBM
    local = pltpu.VMEM

    def turn(value, shift):
        pairs = [
            (run * NEAR + at, run * NEAR + (at + shift) % NEAR)
            for run in range(runs)
            for at in range(NEAR)
        ]
        return lax.ppermute(value, "seq", pairs)

    x, b, c, g = head_input[0], in_matrix[0], out_matrix[0], grad_output[0]
    bias = step_bias.reshape(1, heads)
    logs = decay_log.reshape(1, heads)
    weight = step_weight.T
    packed = call(
        pack_kernel, shape((parts, tokens + heads, width), BF16),
        outside(layer_input[0]), outside(weight),
    )
    whole = lax.all_to_all(packed, "head", 0, 0, tiled=True)
    kept = outside(whole)
    data = call(
        data_kernel,
        (shape((tokens, 2 * wide + 2 * NSTATE), BF16),) * NEAR,
        x, g, b, c,
    )
    received = [outside(data[0])]
    received += [outside(turn(data[shift], shift)) for shift in range(1, NEAR)]
    terms = call(preact_kernel, local((NEAR, each, tokens), F32), whole, weight, bias)
    terms = exchange(terms, "seq", near)
    sent, data, small, states, scaled = call(
        state_kernel,
        (
            local((runs, 2 * wide // runs + EXTRA, NSTATE), BF16),
            local((NEAR, tokens, 2 * wide + 2 * NSTATE), BF16),
            local((4, rows, tokens), F32),
            local((2, NEAR, wide, NSTATE), BF16),
            local((2, NEAR, tokens, wide), BF16),
        ),
        terms, logs, *received, far={index: pltpu.HBM for index in range(2, 2 + NEAR)},
        scratch=(pltpu.SemaphoreType.DMA((NEAR,)),),
    )
    sent = exchange(sent, "seq", far)
    inner, pair, sums = call(
        inner_kernel,
        (
            local((NEAR, tokens, wide), BF16),
            shape((2, NEAR, tokens, NSTATE), BF16),
            local((2, rows, tokens), F32),
        ),
        data, small,
    )
    back = call(far_kernel, local((runs, 2 * wide // runs, NSTATE), BF16), sent)
    back = exchange(back, "seq", far)
    *owned, pre, whole = call(
        last_kernel,
        (shape((tokens, wide + 2 * NSTATE), BF16),) * NEAR + (
            local((count, each, tokens), BF16), local(whole.shape, BF16),
        ),
        back, data, small, states, scaled, inner, outside(pair), sums, kept, far={6: pltpu.HBM, 8: pltpu.HBM},
        scratch=(
            pltpu.VMEM((NEAR, tokens, wide + 2 * NSTATE), BF16),
            pltpu.VMEM(pair.shape, BF16),
            pltpu.SemaphoreType.DMA((2,)),
        ),
    )
    pre = exchange(pre, ("seq", "head"), block)
    part = call(
        part_kernel,
        local((places * shards, heads // shards, LANES), BF16),
        pre, whole,
    )
    part = exchange(part, ("seq", "dp"))
    returned = [owned[0]]
    for shift in range(1, NEAR):
        returned.append(turn(owned[shift], shift))
    grad_input = call(input_kernel, shape((tokens, width), BF16), pre, whole)
    term = call(sum_kernel, shape((heads, LANES // shards), F32), part)
    grad_x, grad_b, grad_c = call(
        final_kernel,
        (shape(x.shape, BF16), shape(b.shape, BF16), shape(c.shape, BF16)),
        outside(term), *returned, far={0: pltpu.HBM},
    )
    return (grad_x[None], grad_b[None], grad_c[None], grad_input[None], term.T)


def solution(mesh):
    in_specs = (P("dp", "seq", "head"),) * 5 + (P(None, "head"), P("head"), P("head"))
    out_specs = (P("dp", "seq", "head"),) * 4 + (P(("seq", "dp"), "head"),)
    return jax.shard_map(body, mesh=mesh, in_specs=in_specs, out_specs=out_specs, check_vma=False)
```
